32 devices in a mesh: row: 4 (over z), col: 8 (over y, x, core).
Axes of the slice: x: 2, y: 2, z: 4, core: 2. Of those that a mesh axis runs over, the one named last changes fastest.
Arguments:
- blocks: float32 [4, 8, 170, 128, 128], P('row', 'col'), may hold values from -1 to 1
- coords: int32 [4, 8, 2, 170], P('row', 'col'), may hold values from 0 to 31, as said below
- vectors: float32 [2, 16384, 128], P(None, ('row', 'col')), may hold values from -6 to 6
Outputs:
- basis: float32 [2, 16384, 128], P(None, ('row', 'col'))
The draws below stay inside these ranges and needn't reach their ends.
Inputs may be any that keep to these rules, and one draw needn't show every extreme that they name: Within each tile the 170 listed positions are distinct, and the positions (0, 0) and (31, 15) are always listed; coords[r, c, 0, k] is below 32 and coords[r, c, 1, k] below 16.
All inputs are finite; a program needn't handle non-finite values.
Results may differ from the reference program's by a relative error of at most 0.0003.
Values sent between devices are 32-bit elements; how exact they have to be, the bound alone decides.
No kernel may reach another device: no remote copies, remote signals or barrier semaphores. Data moves between devices by JAX's collectives and lax.ppermute only.
A program may use at most 192 MiB of HBM per device.

```python
import jax
import jax.numpy as jnp
from jax import lax

BLK = 128
NV = 128
TILE = 2048
APPS = 2
ORDER = 16384
ROWS = 4096
GROUP = 512
NBLK = 170
N_ROW = 4
N_COL = 8


def draw_blocks(key, part):
    shape_all = (N_ROW, N_COL, NBLK, BLK, BLK)
    entries = jax.random.uniform(key, shape_all, jnp.float32, -1.0, 1.0)
    return entries


def draw_coords(key, part):
    block_rows = ROWS // BLK
    block_cols = TILE // BLK
    total_spots = block_rows * block_cols
    key_list = jax.random.split(jax.random.fold_in(key, 5), N_ROW * N_COL)

    def one_tile(tile_key):
        middle = jax.random.permutation(tile_key, total_spots - 2)[:NBLK - 2].astype(jnp.int32) + 1
        chosen = jnp.concatenate([jnp.zeros((1,), jnp.int32), middle, jnp.full((1,), total_spots - 1, jnp.int32)])
        chosen = jax.random.permutation(jax.random.fold_in(tile_key, 3), chosen)
        return jnp.stack([chosen // block_cols, chosen % block_cols])
    return jax.vmap(one_tile)(key_list).reshape(N_ROW, N_COL, 2, NBLK).astype(jnp.int32)


def shard_levels(rng, shape, cuts, smallest, largest):
    gain = 1.0
    for dim, shards_of in cuts:
        draws = jax.random.uniform(jax.random.fold_in(jax.random.fold_in(rng, 6), dim), (shards_of,), jnp.float32, smallest / len(cuts), largest / len(cuts))
        gain = gain * jnp.repeat(jnp.exp(draws), shape[dim] // shards_of).reshape((-1,) + (1,) * (len(shape) - 1 - dim))
    return gain


def normal_values(key, dims, scale, most, pieces=(), kind=jnp.bfloat16):
    values = scale * jax.random.normal(key, dims, jnp.float32)
    if pieces:
        values = values * shard_levels(key, dims, pieces, -0.22, 0.18)
    return jnp.clip(values, -most, most).astype(kind)


def setup_inputs(seed: int = 0) -> dict:
    arg_keys = jax.random.split(jax.random.key(seed), 4)
    blocks = draw_blocks(jax.random.fold_in(arg_keys[3], 71), 0)
    coords = draw_coords(jax.random.fold_in(arg_keys[3], 71), 0)
    vectors = normal_values(arg_keys[2], (2, ORDER, NV), 1.0, 6.0, ((1, 32),), jnp.float32)
    return dict(blocks=blocks, coords=coords, vectors=vectors)


exact_mode = lax.Precision.HIGHEST

def tile_products(values, places, col_side, row_side):
    blk_size = values.shape[1]
    listed = values.shape[0]
    row_blocks = row_side.shape[0] // blk_size
    col_blocks = col_side.shape[0] // blk_size
    row_of = places[0]
    col_of = places[1]
    col_pieces = col_side.reshape(col_blocks, blk_size, -1)[col_of]
    direct = jnp.einsum('kab,kbv->kav', values, col_pieces, precision=exact_mode)
    row_pieces = row_side.reshape(row_blocks, blk_size, -1)[row_of]
    flipped = jnp.einsum('kba,kbv->kav', values, row_pieces, precision=exact_mode)
    row_hot = (row_of[None, :] == jnp.arange(row_blocks, dtype=jnp.int32)[:, None]).astype(values.dtype)
    col_hot = (col_of[None, :] == jnp.arange(col_blocks, dtype=jnp.int32)[:, None]).astype(values.dtype)
    out_rows = jnp.dot(row_hot, direct.reshape(listed, -1), precision=exact_mode).reshape(row_side.shape[0], -1)
    out_cols = jnp.dot(col_hot, flipped.reshape(listed, -1), precision=exact_mode).reshape(col_side.shape[0], -1)
    return (out_rows, out_cols)

def normal_basis(applied, factor):
    return lax.linalg.triangular_solve(factor, applied, left_side=False, lower=True, transpose_a=True)

def apply_full(upper, lower, blocks, coords):
    upper_grid = upper.reshape(N_ROW, N_COL, GROUP, NV)
    lower_grid = lower.reshape(N_ROW, N_COL, GROUP, NV)

    def visit_tile(carry, tile_item):
        sum_upper, sum_lower = carry
        values, places, flat_id = tile_item
        row_id = flat_id // N_COL
        col_id = flat_id % N_COL
        col_side = lax.dynamic_index_in_dim(lower_grid, col_id, 1, keepdims=False).reshape(TILE, NV)
        row_side = lax.dynamic_index_in_dim(upper_grid, row_id, 0, keepdims=False).reshape(ROWS, NV)
        out_rows, out_cols = tile_products(values, places, col_side, row_side)
        sum_upper = sum_upper.at[row_id].add(out_rows.reshape(N_COL, GROUP, NV))
        sum_lower = sum_lower.at[:, col_id].add(out_cols.reshape(N_ROW, GROUP, NV))
        return ((sum_upper, sum_lower), None)
    start_sum = jnp.zeros((N_ROW, N_COL, GROUP, NV), jnp.float32)
    flat_ids = jnp.arange(N_ROW * N_COL, dtype=jnp.int32)
    summed, unused = lax.scan(visit_tile, (start_sum, start_sum), (blocks.reshape(N_ROW * N_COL, NBLK, BLK, BLK), coords.reshape(N_ROW * N_COL, 2, NBLK), flat_ids))
    return (summed[0].reshape(ORDER, NV), summed[1].reshape(ORDER, NV))

def reference(blocks, coords, vectors):
    upper = vectors[0]
    lower = vectors[1]
    for app_index in range(APPS):
        new_upper, new_lower = apply_full(upper, lower, blocks, coords)
        gram_sum = (jnp.einsum('nv,nw->vw', new_upper, new_upper, precision=exact_mode) + jnp.einsum('nv,nw->vw', new_lower, new_lower, precision=exact_mode)) / (2 * ORDER)
        factor = jnp.linalg.cholesky(gram_sum)
        upper = normal_basis(new_upper, factor)
        lower = normal_basis(new_lower, factor)
    return jnp.stack([upper, lower])
```

```python
import functools

import jax
import jax.numpy as jnp
from jax import lax
from jax.experimental import pallas as pl
from jax.experimental.pallas import tpu as pltpu
from jax.sharding import PartitionSpec as P


f32 = jnp.float32
bf16 = jnp.bfloat16
exact_mode = lax.Precision.HIGHEST


def halves(x):
    hi = x.astype(bf16)
    return hi, (x - hi.astype(f32)).astype(bf16)


def swap(x, axis, mask):
    size = lax.axis_size(axis)
    return lax.ppermute(x, axis, [(i, i ^ mask) for i in range(size)])


def chunk_of(listed):
    for size in range(min(listed, 17), 0, -1):
        if listed % size == 0:
            return size
    return 1


def tile_kernel(
    places, here, values_ref, *rest, flipped, in_shards, out_shards, listed, step_blocks, group_blocks
):
    n_in = len(in_shards)
    n_out = len(out_shards)
    in_refs = rest[:n_in]
    out_refs = rest[n_in : n_in + n_out]
    stacked, acc = rest[n_in + n_out :]
    blk = values_ref.shape[1]
    step = pl.program_id(0)

    @pl.when(step == 0)
    def _():
        acc[...] = jnp.zeros_like(acc)
        for ref, shards in zip(in_refs, in_shards):
            for place, mask in enumerate(shards):
                first = (here[0] ^ mask) * group_blocks
                for g in range(group_blocks):
                    hi, lo = halves(ref[pl.ds((place * group_blocks + g) * blk, blk), :])
                    both = jnp.concatenate([hi, lo], axis=1)
                    stacked[first + g, 0:blk, :] = both
                    stacked[first + g, blk : 2 * blk, :] = both

    sums = []
    for q in range(step_blocks):
        k = step * step_blocks + q
        i = places[0, k]
        j = places[1, k]
        source, target = (i, j) if flipped else (j, i)
        entry = values_ref[q]
        hi, lo = halves(entry.T if flipped else entry)
        p = jnp.dot(
            jnp.concatenate([hi, lo], axis=1), stacked[source], preferred_element_type=f32
        )
        nv = p.shape[1] // 2
        sums.append((target, p[:, :nv] + p[:, nv:]))
    for target, p in sums:
        acc[target] = acc[target] + p

    @pl.when(step == listed // step_blocks - 1)
    def _():
        for ref, shards in zip(out_refs, out_shards):
            for place, mask in enumerate(shards):
                first = (here[1] ^ mask) * group_blocks
                for g in range(group_blocks):
                    ref[pl.ds((place * group_blocks + g) * blk, blk), :] = acc[first + g]


def tile_products(values, places, here, pieces, in_shards, out_shards, flipped):
    listed, blk, _ = values.shape
    nv = pieces[0].shape[1]
    group = pieces[0].shape[0] // len(in_shards[0])
    group_blocks = group // blk
    step_blocks = chunk_of(listed)
    n_in = sum(len(s) for s in in_shards) * group_blocks
    n_out = sum(len(s) for s in out_shards) * group_blocks
    whole = lambda shape: pl.BlockSpec(shape, lambda g, *_: (0, 0))
    out_shapes = [(len(s) * group, nv) for s in out_shards]
    body = functools.partial(
        tile_kernel,
        flipped=flipped,
        in_shards=in_shards,
        out_shards=out_shards,
        listed=listed,
        step_blocks=step_blocks,
        group_blocks=group_blocks,
    )
    return pl.pallas_call(
        body,
        name="tile_flipped" if flipped else "tile_direct",
        out_shape=[jax.ShapeDtypeStruct(s, f32) for s in out_shapes],
        grid_spec=pltpu.PrefetchScalarGridSpec(
            num_scalar_prefetch=2,
            grid=(listed // step_blocks,),
            in_specs=[pl.BlockSpec((step_blocks, blk, blk), lambda g, *_: (g, 0, 0))]
            + [whole(p.shape) for p in pieces],
            out_specs=[whole(s) for s in out_shapes],
            scratch_shapes=[
                pltpu.VMEM((n_in, 2 * blk, 2 * nv), bf16),
                pltpu.VMEM((n_out, blk, nv), f32),
            ],
        ),
        cost_estimate=pl.CostEstimate(
            flops=2 * listed * blk * blk * nv * 4, transcendentals=0, bytes_accessed=values.size * 4
        ),
    )(places, here, values, *pieces)


def gram_kernel(here, *rest, n_upper, n_lower, scale):
    upper_refs = rest[:n_upper]
    lower_refs = rest[n_upper : n_upper + n_lower]
    rest = rest[n_upper + n_lower :]
    if scale:
        w_ref, y_ref, mine_ref, other_ref, full = rest
    else:
        mine_ref, other_ref, full = rest
    total = None
    for band, refs in enumerate((upper_refs, lower_refs)):
        y = refs[0][...]
        for r in refs[1:]:
            y = y + r[...]
        if scale:
            y = jnp.dot(y, w_ref[...], precision=exact_mode, preferred_element_type=f32)
            y_ref[band] = y
        part = lax.dot_general(
            y, y, (((0,), (0,)), ((), ())), precision=exact_mode, preferred_element_type=f32
        )
        total = part if total is None else total + part
    full[...] = total
    half = total.shape[0] // 2
    mine_ref[...] = full[pl.ds(here[0] * half, half), :]
    other_ref[...] = full[pl.ds((1 - here[0]) * half, half), :]


def gram_parts(parity, uppers, lowers, weight=None):
    rows, nv = uppers[0].shape
    half = jax.ShapeDtypeStruct((nv // 2, nv), f32)
    out_shape = [half, half]
    args = list(uppers) + list(lowers)
    if weight is not None:
        out_shape = [jax.ShapeDtypeStruct((2, rows, nv), f32)] + out_shape
        args.append(weight)
    vmem = pl.BlockSpec(memory_space=pltpu.VMEM)
    return pl.pallas_call(
        functools.partial(
            gram_kernel, n_upper=len(uppers), n_lower=len(lowers), scale=weight is not None
        ),
        name="gram_scaled" if weight is not None else "gram_plain",
        out_shape=out_shape,
        in_specs=[pl.BlockSpec(memory_space=pltpu.SMEM)] + [vmem] * len(args),
        out_specs=[vmem] * len(out_shape),
        scratch_shapes=[pltpu.VMEM((nv, nv), f32)],
    )(parity, *args)


def factor_kernel(here, *rest, n_own, total_rows, apply):
    own_refs = rest[:n_own]
    other_ref = rest[n_own]
    rest = rest[n_own + 1 :]
    if apply:
        y_ref, out_ref, full = rest
    else:
        w_ref, full = rest
    size = full.shape[0]
    half = size // 2
    own = own_refs[0][...]
    for r in own_refs[1:]:
        own = own + r[...]
    full[pl.ds(here[0] * half, half), :] = own
    full[pl.ds((1 - here[0]) * half, half), :] = other_ref[...]
    sub = 8
    inv_rows = 1.0 / total_rows
    lane = lax.broadcasted_iota(jnp.int32, (sub, size), 1)
    row_in = lax.broadcasted_iota(jnp.int32, (sub, size), 0)
    m = [full[pl.ds(g * sub, sub), :] * inv_rows for g in range(size // sub)]
    for k in range(size):
        g0, s0 = divmod(k, sub)
        at_k = lane == k
        row = m[g0][s0 : s0 + 1, :]
        pivot = row[:, k : k + 1]
        scaled = jnp.where(at_k, 1.0, jnp.broadcast_to(row, (sub, size))) * jnp.broadcast_to(
            1.0 / pivot, (sub, size)
        )
        for g in range(g0, size // sub):
            if g == g0 and s0 == sub - 1:
                continue
            col = jnp.broadcast_to(m[g][:, k : k + 1], (sub, size))
            new = jnp.where(at_k, 0.0, m[g]) - col * scaled
            m[g] = jnp.where(row_in > s0, new, m[g]) if g == g0 else new
    for g in range(size // sub):
        diag = lane == row_in + g * sub
        d = jnp.sum(jnp.where(diag, m[g], 0.0), axis=1, keepdims=True)
        unit = jnp.where(diag, 1.0, jnp.where(lane < row_in + g * sub, m[g], 0.0))
        full[pl.ds(g * sub, sub), :] = unit * lax.rsqrt(d)
    if apply:
        w = full[...]
        for band in range(2):
            out_ref[band] = lax.dot_general(
                y_ref[band],
                w,
                (((1,), (1,)), ((), ())),
                precision=exact_mode,
                preferred_element_type=f32,
            )
    else:
        w_ref[...] = full[...].T


def factor_inverse(parity, own, other, total_rows, applied=None):
    half, nv = other.shape
    vmem = pl.BlockSpec(memory_space=pltpu.VMEM)
    args = list(own) + [other]
    if applied is None:
        out_shape = jax.ShapeDtypeStruct((nv, nv), f32)
    else:
        out_shape = jax.ShapeDtypeStruct(applied.shape, f32)
        args.append(applied)
    return pl.pallas_call(
        functools.partial(
            factor_kernel, n_own=len(own), total_rows=total_rows, apply=applied is not None
        ),
        name="factor" if applied is None else "factor_apply",
        out_shape=out_shape,
        in_specs=[pl.BlockSpec(memory_space=pltpu.SMEM)] + [vmem] * len(args),
        out_specs=vmem,
        scratch_shapes=[pltpu.VMEM((nv, nv), f32)],
    )(parity, *args)


def local(blocks, coords, vectors):
    n_row = lax.axis_size("row")
    n_col = lax.axis_size("col")
    group = vectors.shape[1]
    total_rows = 2 * group * n_row * n_col
    values = blocks.reshape(blocks.shape[2], blocks.shape[3], blocks.shape[4])
    places = coords.reshape(2, coords.shape[3])
    row_id = lax.axis_index("row")
    col_id = lax.axis_index("col")
    here_direct = jnp.stack([row_id, col_id]).astype(jnp.int32)
    here_flipped = jnp.stack([col_id, row_id]).astype(jnp.int32)
    parity = (col_id & 1).astype(jnp.int32).reshape(1)
    even = list(range(2, n_col, 2))
    row_masks = list(range(1, n_row))

    def spread_row(x):
        return [x] + [swap(x, "row", m) for m in row_masks]

    def spread_col(x):
        far = [swap(x, "col", m) for m in even]
        near = swap(x, "col", 1)
        joined = [swap(f, "col", 1) for f in far]
        return [x, near] + far + joined

    row_shards = [[0]] + [[m] for m in row_masks]
    col_shards = [[0], [1]] + [[m] for m in even] + [[m ^ 1] for m in even]
    col_out = [[0] + even, [m ^ 1 for m in [0] + even]]

    def direct(col_band):
        return tile_products(values, places, here_direct, spread_row(col_band), row_shards, col_out, False)

    def flipped(row_band):
        return tile_products(values, places, here_flipped, spread_col(row_band), col_shards, row_shards, True)

    def gather_col(outs):
        mine, others = outs
        both = mine + swap(others, "col", 1)
        parts = [both[i * group : (i + 1) * group] for i in range(len(even) + 1)]
        return [parts[0]] + [swap(p, "col", m) for p, m in zip(parts[1:], even)]

    def gather_row(outs):
        return [outs[0]] + [swap(p, "row", m) for p, m in zip(outs[1:], row_masks)]

    def reduce_gram(mine, other):
        own = mine + swap(other, "col", 1)
        own = functools.reduce(jnp.add, [own] + [swap(own, "col", m) for m in even])
        parts = [own] + [swap(own, "row", m) for m in row_masks]
        own = functools.reduce(jnp.add, parts)
        return [own], swap(own, "col", 1)

    upper, lower = vectors[0], vectors[1]
    lower1 = functools.reduce(jnp.add, gather_row(flipped(upper)))
    upper1 = functools.reduce(jnp.add, gather_col(direct(lower)))
    weight = factor_inverse(parity, *reduce_gram(*gram_parts(parity, [upper1], [lower1])), total_rows)
    uppers = gather_col(direct(lower1))
    lowers = gather_row(flipped(upper1))
    applied, mine, other = gram_parts(parity, uppers, lowers, weight)
    return factor_inverse(parity, *reduce_gram(mine, other), total_rows, applied)


def solution(mesh):
    return jax.shard_map(
        local,
        mesh=mesh,
        in_specs=(
            P("row", "col", None, None, None),
            P("row", "col", None, None),
            P(None, ("row", "col"), None),
        ),
        out_specs=P(None, ("row", "col"), None),
        check_vma=False,
    )
```

```python
import functools

import jax
import jax.numpy as jnp
from jax import lax
from jax.experimental import pallas as pl
from jax.experimental.pallas import tpu as pltpu
from jax.sharding import PartitionSpec as P


f32 = jnp.float32
bf16 = jnp.bfloat16
exact_mode = lax.Precision.HIGHEST


def halves(x):
    hi = x.astype(bf16)
    return hi, (x - hi.astype(f32)).astype(bf16)


def swap(x, axis, mask):
    size = lax.axis_size(axis)
    return lax.ppermute(x, axis, [(i, i ^ mask) for i in range(size)])


def chunk_of(listed):
    for size in range(min(listed, 17), 0, -1):
        if listed % size == 0:
            return size
    return 1


def tile_kernel(
    places, here, values_ref, *rest, flipped, in_shards, out_shards, listed, step_blocks, group_blocks
):
    n_in = len(in_shards)
    n_out = len(out_shards)
    in_refs = rest[:n_in]
    out_refs = rest[n_in : n_in + n_out]
    stacked, acc = rest[n_in + n_out :]
    blk = values_ref.shape[1]
    step = pl.program_id(0)

    @pl.when(step == 0)
    def _():
        acc[...] = jnp.zeros_like(acc)
        for ref, shards in zip(in_refs, in_shards):
            for place, mask in enumerate(shards):
                first = (here[0] ^ mask) * group_blocks
                for g in range(group_blocks):
                    hi, lo = halves(ref[pl.ds((place * group_blocks + g) * blk, blk), :])
                    both = jnp.concatenate([hi, lo], axis=1)
                    stacked[first + g, 0:blk, :] = both
                    stacked[first + g, blk : 2 * blk, :] = both

    sums = []
    for q in range(step_blocks):
        k = step * step_blocks + q
        i = places[0, k]
        j = places[1, k]
        source, target = (i, j) if flipped else (j, i)
        entry = values_ref[q]
        hi, lo = halves(entry.T if flipped else entry)
        p = jnp.dot(
            jnp.concatenate([hi, lo], axis=1), stacked[source], preferred_element_type=f32
        )
        nv = p.shape[1] // 2
        sums.append((target, p[:, :nv] + p[:, nv:]))
    for target, p in sums:
        acc[target] = acc[target] + p

    @pl.when(step == listed // step_blocks - 1)
    def _():
        for ref, shards in zip(out_refs, out_shards):
            for place, mask in enumerate(shards):
                first = (here[1] ^ mask) * group_blocks
                for g in range(group_blocks):
                    ref[pl.ds((place * group_blocks + g) * blk, blk), :] = acc[first + g]


def tile_products(values, places, here, pieces, in_shards, out_shards, flipped):
    listed, blk, _ = values.shape
    nv = pieces[0].shape[1]
    group = pieces[0].shape[0] // len(in_shards[0])
    group_blocks = group // blk
    step_blocks = chunk_of(listed)
    n_in = sum(len(s) for s in in_shards) * group_blocks
    n_out = sum(len(s) for s in out_shards) * group_blocks
    whole = lambda shape: pl.BlockSpec(shape, lambda g, *_: (0, 0))
    out_shapes = [(len(s) * group, nv) for s in out_shards]
    body = functools.partial(
        tile_kernel,
        flipped=flipped,
        in_shards=in_shards,
        out_shards=out_shards,
        listed=listed,
        step_blocks=step_blocks,
        group_blocks=group_blocks,
    )
    return pl.pallas_call(
        body,
        name="tile_flipped" if flipped else "tile_direct",
        out_shape=[jax.ShapeDtypeStruct(s, f32) for s in out_shapes],
        grid_spec=pltpu.PrefetchScalarGridSpec(
            num_scalar_prefetch=2,
            grid=(listed // step_blocks,),
            in_specs=[pl.BlockSpec((step_blocks, blk, blk), lambda g, *_: (g, 0, 0))]
            + [whole(p.shape) for p in pieces],
            out_specs=[whole(s) for s in out_shapes],
            scratch_shapes=[
                pltpu.VMEM((n_in, 2 * blk, 2 * nv), bf16),
                pltpu.VMEM((n_out, blk, nv), f32),
            ],
        ),
        cost_estimate=pl.CostEstimate(
            flops=2 * listed * blk * blk * nv * 4, transcendentals=0, bytes_accessed=values.size * 4
        ),
    )(places, here, values, *pieces)


def gram_kernel(here, *rest, n_upper, n_lower, scale):
    upper_refs = rest[:n_upper]
    lower_refs = rest[n_upper : n_upper + n_lower]
    rest = rest[n_upper + n_lower :]
    if scale:
        w_ref, y_ref, mine_ref, other_ref, full = rest
    else:
        mine_ref, other_ref, full = rest
    total = None
    for band, refs in enumerate((upper_refs, lower_refs)):
        y = refs[0][...]
        for r in refs[1:]:
            y = y + r[...]
        if scale:
            y = jnp.dot(y, w_ref[...], precision=exact_mode, preferred_element_type=f32)
            y_ref[band] = y
        part = lax.dot_general(
            y, y, (((0,), (0,)), ((), ())), precision=exact_mode, preferred_element_type=f32
        )
        total = part if total is None else total + part
    full[...] = total
    half = total.shape[0] // 2
    mine_ref[...] = full[pl.ds(here[0] * half, half), :]
    other_ref[...] = full[pl.ds((1 - here[0]) * half, half), :]


def gram_parts(parity, uppers, lowers, weight=None):
    rows, nv = uppers[0].shape
    half = jax.ShapeDtypeStruct((nv // 2, nv), f32)
    out_shape = [half, half]
    args = list(uppers) + list(lowers)
    if weight is not None:
        out_shape = [jax.ShapeDtypeStruct((2, rows, nv), f32)] + out_shape
        args.append(weight)
    vmem = pl.BlockSpec(memory_space=pltpu.VMEM)
    return pl.pallas_call(
        functools.partial(
            gram_kernel, n_upper=len(uppers), n_lower=len(lowers), scale=weight is not None
        ),
        name="gram_scaled" if weight is not None else "gram_plain",
        out_shape=out_shape,
        in_specs=[pl.BlockSpec(memory_space=pltpu.SMEM)] + [vmem] * len(args),
        out_specs=[vmem] * len(out_shape),
        scratch_shapes=[pltpu.VMEM((nv, nv), f32)],
    )(parity, *args)


def factor_kernel(here, *rest, n_own, total_rows, apply):
    own_refs = rest[:n_own]
    other_ref = rest[n_own]
    rest = rest[n_own + 1 :]
    if apply:
        y_ref, out_ref, full = rest
    else:
        w_ref, full = rest
    size = full.shape[0]
    half = size // 2
    own = own_refs[0][...]
    for r in own_refs[1:]:
        own = own + r[...]
    full[pl.ds(here[0] * half, half), :] = own
    full[pl.ds((1 - here[0]) * half, half), :] = other_ref[...]
    sub = 8
    inv_rows = 1.0 / total_rows
    lane = lax.broadcasted_iota(jnp.int32, (sub, size), 1)
    row_in = lax.broadcasted_iota(jnp.int32, (sub, size), 0)
    m = [full[pl.ds(g * sub, sub), :] * inv_rows for g in range(size // sub)]
    for k in range(size):
        g0, s0 = divmod(k, sub)
        at_k = lane == k
        row = m[g0][s0 : s0 + 1, :]
        pivot = row[:, k : k + 1]
        scaled = jnp.where(at_k, 1.0, jnp.broadcast_to(row, (sub, size))) * jnp.broadcast_to(
            1.0 / pivot, (sub, size)
        )
        for g in range(g0, size // sub):
            if g == g0 and s0 == sub - 1:
                continue
            col = jnp.broadcast_to(m[g][:, k : k + 1], (sub, size))
            new = jnp.where(at_k, 0.0, m[g]) - col * scaled
            m[g] = jnp.where(row_in > s0, new, m[g]) if g == g0 else new
    for g in range(size // sub):
        diag = lane == row_in + g * sub
        d = jnp.sum(jnp.where(diag, m[g], 0.0), axis=1, keepdims=True)
        unit = jnp.where(diag, 1.0, jnp.where(lane < row_in + g * sub, m[g], 0.0))
        full[pl.ds(g * sub, sub), :] = unit * lax.rsqrt(d)
    if apply:
        w = full[...]
        for band in range(2):
            out_ref[band] = lax.dot_general(
                y_ref[band],
                w,
                (((1,), (1,)), ((), ())),
                precision=exact_mode,
                preferred_element_type=f32,
            )
    else:
        w_ref[...] = full[...].T


def factor_inverse(parity, own, other, total_rows, applied=None):
    _, nv = other.shape
    vmem = pl.BlockSpec(memory_space=pltpu.VMEM)
    args = list(own) + [other]
    if applied is None:
        out_shape = jax.ShapeDtypeStruct((nv, nv), f32)
    else:
        out_shape = jax.ShapeDtypeStruct(applied.shape, f32)
        args.append(applied)
    return pl.pallas_call(
        functools.partial(
            factor_kernel, n_own=len(own), total_rows=total_rows, apply=applied is not None
        ),
        name="factor" if applied is None else "factor_apply",
        out_shape=out_shape,
        in_specs=[pl.BlockSpec(memory_space=pltpu.SMEM)] + [vmem] * len(args),
        out_specs=vmem,
        scratch_shapes=[pltpu.VMEM((nv, nv), f32)],
    )(parity, *args)


def local(blocks, coords, vectors):
    n_row = lax.axis_size("row")
    n_col = lax.axis_size("col")
    group = vectors.shape[1]
    total_rows = 2 * group * n_row * n_col
    values = blocks.reshape(blocks.shape[2], blocks.shape[3], blocks.shape[4])
    places = coords.reshape(2, coords.shape[3])
    row_id = lax.axis_index("row")
    col_id = lax.axis_index("col")
    here_direct = jnp.stack([row_id, col_id]).astype(jnp.int32)
    here_flipped = jnp.stack([col_id, row_id]).astype(jnp.int32)
    parity = (col_id & 1).astype(jnp.int32).reshape(1)
    even = list(range(2, n_col, 2))
    row_masks = list(range(1, n_row))

    def spread_row(x):
        return [x] + [swap(x, "row", m) for m in row_masks]

    def spread_col(x):
        far = [swap(x, "col", m) for m in even]
        near = swap(x, "col", 1)
        joined = [swap(f, "col", 1) for f in far]
        return [x, near] + far + joined

    row_shards = [[0]] + [[m] for m in row_masks]
    col_shards = [[0], [1]] + [[m] for m in even] + [[m ^ 1] for m in even]
    col_out = [[0] + even, [m ^ 1 for m in [0] + even]]

    def direct(pieces):
        return tile_products(values, places, here_direct, pieces, row_shards, col_out, False)

    def flipped(pieces):
        return tile_products(values, places, here_flipped, pieces, col_shards, row_shards, True)

    def gather_col(outs):
        mine, others = outs
        both = mine + swap(others, "col", 1)
        parts = [both[i * group : (i + 1) * group] for i in range(len(even) + 1)]
        return [parts[0]] + [swap(p, "col", m) for p, m in zip(parts[1:], even)]

    def gather_row(outs):
        return [outs[0]] + [swap(p, "row", m) for p, m in zip(outs[1:], row_masks)]

    def reduce_gram(mine, other):
        own = mine + swap(other, "col", 1)
        own = functools.reduce(jnp.add, [own] + [swap(own, "col", m) for m in even])
        parts = [own] + [swap(own, "row", m) for m in row_masks]
        own = functools.reduce(jnp.add, parts)
        return [own], swap(own, "col", 1)

    upper, lower = vectors[0], vectors[1]
    pieces_z = spread_row(lower)
    lower1 = functools.reduce(jnp.add, gather_row(flipped(spread_col(upper))))
    upper1 = functools.reduce(jnp.add, gather_col(direct(pieces_z)))
    pieces_z = spread_row(lower1)
    lowers = gather_row(flipped(spread_col(upper1)))
    parts = gram_parts(parity, [upper1], [lower1])
    parts = reduce_gram(*parts)
    weight = factor_inverse(parity, *parts, total_rows)
    uppers = gather_col(direct(pieces_z))
    applied, mine, other = gram_parts(parity, uppers, lowers, weight)
    parts = reduce_gram(mine, other)
    return factor_inverse(parity, *parts, total_rows, applied)


def solution(mesh):
    return jax.shard_map(
        local,
        mesh=mesh,
        in_specs=(
            P("row", "col", None, None, None),
            P("row", "col", None, None),
            P(None, ("row", "col"), None),
        ),
        out_specs=P(None, ("row", "col"), None),
        check_vma=False,
    )
```

```python
import functools

import jax
import jax.numpy as jnp
from jax import lax
from jax.experimental import pallas as pl
from jax.experimental.pallas import tpu as pltpu
from jax.sharding import PartitionSpec as P


f32 = jnp.float32
bf16 = jnp.bfloat16
exact_mode = lax.Precision.HIGHEST


def halves(x):
    hi = x.astype(bf16)
    return hi, (x - hi.astype(f32)).astype(bf16)


def swap(x, axis, mask):
    size = lax.axis_size(axis)
    return lax.ppermute(x, axis, [(i, i ^ mask) for i in range(size)])


def chunk_of(listed):
    for size in range(min(listed, 17), 0, -1):
        if listed % size == 0:
            return size
    return 1


def tile_kernel(
    places, here, values_ref, *rest, flipped, in_shards, out_shards, listed, step_blocks, group_blocks
):
    n_in = len(in_shards)
    n_out = len(out_shards)
    in_refs = rest[:n_in]
    out_refs = rest[n_in : n_in + n_out]
    stacked, acc = rest[n_in + n_out :]
    blk = values_ref.shape[1]
    step = pl.program_id(0)

    @pl.when(step == 0)
    def _():
        acc[...] = jnp.zeros_like(acc)
        for ref, shards in zip(in_refs, in_shards):
            for place, mask in enumerate(shards):
                first = (here[0] ^ mask) * group_blocks
                for g in range(group_blocks):
                    hi, lo = halves(ref[pl.ds((place * group_blocks + g) * blk, blk), :])
                    both = jnp.concatenate([hi, lo], axis=1)
                    stacked[first + g, 0:blk, :] = both
                    stacked[first + g, blk : 2 * blk, :] = both

    sums = []
    for q in range(step_blocks):
        k = step * step_blocks + q
        i = places[0, k]
        j = places[1, k]
        source, target = (i, j) if flipped else (j, i)
        entry = values_ref[q]
        hi, lo = halves(entry.T if flipped else entry)
        p = jnp.dot(
            jnp.concatenate([hi, lo], axis=1), stacked[source], preferred_element_type=f32
        )
        nv = p.shape[1] // 2
        sums.append((target, p[:, :nv] + p[:, nv:]))
    for target, p in sums:
        acc[target] = acc[target] + p

    @pl.when(step == listed // step_blocks - 1)
    def _():
        for ref, shards in zip(out_refs, out_shards):
            for place, mask in enumerate(shards):
                first = (here[1] ^ mask) * group_blocks
                for g in range(group_blocks):
                    ref[pl.ds((place * group_blocks + g) * blk, blk), :] = acc[first + g]


def tile_products(values, places, here, pieces, in_shards, out_shards, flipped):
    listed, blk, _ = values.shape
    nv = pieces[0].shape[1]
    group = pieces[0].shape[0] // len(in_shards[0])
    group_blocks = group // blk
    step_blocks = chunk_of(listed)
    n_in = sum(len(s) for s in in_shards) * group_blocks
    n_out = sum(len(s) for s in out_shards) * group_blocks
    whole = lambda shape: pl.BlockSpec(shape, lambda g, *_: (0, 0))
    out_shapes = [(len(s) * group, nv) for s in out_shards]
    body = functools.partial(
        tile_kernel,
        flipped=flipped,
        in_shards=in_shards,
        out_shards=out_shards,
        listed=listed,
        step_blocks=step_blocks,
        group_blocks=group_blocks,
    )
    return pl.pallas_call(
        body,
        name="tile_flipped" if flipped else "tile_direct",
        out_shape=[jax.ShapeDtypeStruct(s, f32) for s in out_shapes],
        grid_spec=pltpu.PrefetchScalarGridSpec(
            num_scalar_prefetch=2,
            grid=(listed // step_blocks,),
            in_specs=[pl.BlockSpec((step_blocks, blk, blk), lambda g, *_: (g, 0, 0))]
            + [whole(p.shape) for p in pieces],
            out_specs=[whole(s) for s in out_shapes],
            scratch_shapes=[
                pltpu.VMEM((n_in, 2 * blk, 2 * nv), bf16),
                pltpu.VMEM((n_out, blk, nv), f32),
            ],
        ),
        cost_estimate=pl.CostEstimate(
            flops=2 * listed * blk * blk * nv * 4, transcendentals=0, bytes_accessed=values.size * 4
        ),
    )(places, here, values, *pieces)


def gram_kernel(here, *rest, n_upper, n_lower, scale):
    upper_refs = rest[:n_upper]
    lower_refs = rest[n_upper : n_upper + n_lower]
    rest = rest[n_upper + n_lower :]
    if scale:
        w_ref, y_ref, mine_ref, other_ref, full = rest
    else:
        mine_ref, other_ref, full = rest
    total = None
    for band, refs in enumerate((upper_refs, lower_refs)):
        y = refs[0][...]
        for r in refs[1:]:
            y = y + r[...]
        if scale:
            y = jnp.dot(y, w_ref[...], precision=exact_mode, preferred_element_type=f32)
            y_ref[band] = y
        part = lax.dot_general(
            y, y, (((0,), (0,)), ((), ())), precision=exact_mode, preferred_element_type=f32
        )
        total = part if total is None else total + part
    full[...] = total
    half = total.shape[0] // 2
    mine_ref[...] = full[pl.ds(here[0] * half, half), :]
    other_ref[...] = full[pl.ds((1 - here[0]) * half, half), :]


def gram_parts(parity, uppers, lowers, weight=None):
    rows, nv = uppers[0].shape
    half = jax.ShapeDtypeStruct((nv // 2, nv), f32)
    out_shape = [half, half]
    args = list(uppers) + list(lowers)
    if weight is not None:
        out_shape = [jax.ShapeDtypeStruct((2, rows, nv), f32)] + out_shape
        args.append(weight)
    vmem = pl.BlockSpec(memory_space=pltpu.VMEM)
    return pl.pallas_call(
        functools.partial(
            gram_kernel, n_upper=len(uppers), n_lower=len(lowers), scale=weight is not None
        ),
        name="gram_scaled" if weight is not None else "gram_plain",
        out_shape=out_shape,
        in_specs=[pl.BlockSpec(memory_space=pltpu.SMEM)] + [vmem] * len(args),
        out_specs=[vmem] * len(out_shape),
        scratch_shapes=[pltpu.VMEM((nv, nv), f32)],
    )(parity, *args)


def factor_kernel(here, *rest, n_own, total_rows, apply):
    own_refs = rest[:n_own]
    other_ref = rest[n_own]
    rest = rest[n_own + 1 :]
    if apply:
        y_ref, out_ref, full, rows = rest
    else:
        w_ref, full, rows = rest
    size = full.shape[0]
    half = size // 2
    own = own_refs[0][...]
    for r in own_refs[1:]:
        own = own + r[...]
    full[pl.ds(here[0] * half, half), :] = own
    full[pl.ds((1 - here[0]) * half, half), :] = other_ref[...]
    sub = 8
    groups = size // sub
    lane = lax.broadcasted_iota(jnp.int32, (sub, size), 1)
    row_in = lax.broadcasted_iota(jnp.int32, (sub, size), 0)

    def spread(x, k):
        return jnp.broadcast_to(x[:, k : k + 1], (sub, size))

    m = [full[pl.ds(g * sub, sub), :] for g in range(groups)]
    kept = [jnp.where(lane == row_in + g * sub, m[g], 0.0) for g in range(groups)]
    across = functools.reduce(jnp.add, [jnp.sum(x, axis=0, keepdims=True) for x in kept])
    inv_rows = 1.0 / total_rows
    unit_row = lax.rsqrt(across * inv_rows)
    for g in range(groups):
        unit_col = lax.rsqrt(jnp.sum(kept[g], axis=1, keepdims=True) * inv_rows)
        m[g] = (m[g] * inv_rows * unit_row) * unit_col

    for g0 in range(groups):
        k = g0 * sub
        rows[pl.ds(k, sub), :] = m[g0]
        r = [rows[pl.ds(k + i, sub, stride=0), :] for i in range(sub)]
        s = {(i, j): spread(r[i], k + j) for i in range(sub) for j in range(i, sub)}
        in_panel = (lane >= k) & (lane < k + sub)
        done = lane < k + sub
        r = [jnp.where(lane == k + i, 1.0, jnp.where(in_panel, 0.0, r[i])) for i in range(sub)]
        f = [None] * sub
        q = {}
        for i in range(0, sub, 2):
            a, b, c = s[i, i], s[i, i + 1], s[i + 1, i + 1]
            inv = 1.0 / (a * c - b * b)
            t = b / a
            first = jnp.where(done, r[i], 0.0) * lax.rsqrt(a)
            second = jnp.where(done, r[i + 1] - t * r[i], 0.0) * lax.rsqrt(c - b * t)
            full[pl.ds(k + i, 1), :] = first[0:1]
            full[pl.ds(k + i + 1, 1), :] = second[0:1]
            a, b, c = a * inv, b * inv, c * inv
            f[i] = c * r[i] - b * r[i + 1]
            f[i + 1] = a * r[i + 1] - b * r[i]
            for j in range(i + 2, sub):
                q[i, j] = c * s[i, j] - b * s[i + 1, j]
                q[i + 1, j] = a * s[i + 1, j] - b * s[i, j]
            for j in range(i + 2, sub):
                r[j] = r[j] - (s[i, j] * f[i] + s[i + 1, j] * f[i + 1])
                for l in range(j, sub):
                    s[j, l] = s[j, l] - (s[i, j] * q[i, l] + s[i + 1, j] * q[i + 1, l])
        for i in range(sub - 4, -1, -2):
            for j in range(i + 2, sub):
                f[i] = f[i] - q[i, j] * f[j]
                f[i + 1] = f[i + 1] - q[i + 1, j] * f[j]
        for g in range(g0 + 1, groups):
            change = spread(m[g], k) * f[0]
            for j in range(1, sub):
                change = change + spread(m[g], k + j) * f[j]
            m[g] = jnp.where(in_panel, 0.0, m[g]) - change

    inverse = full[...] * unit_row
    if apply:
        for band in range(2):
            out_ref[band] = lax.dot_general(
                y_ref[band],
                inverse,
                (((1,), (1,)), ((), ())),
                precision=exact_mode,
                preferred_element_type=f32,
            )
    else:
        w_ref[...] = inverse.T


def factor_inverse(parity, own, other, total_rows, applied=None):
    _, nv = other.shape
    vmem = pl.BlockSpec(memory_space=pltpu.VMEM)
    args = list(own) + [other]
    if applied is None:
        out_shape = jax.ShapeDtypeStruct((nv, nv), f32)
    else:
        out_shape = jax.ShapeDtypeStruct(applied.shape, f32)
        args.append(applied)
    return pl.pallas_call(
        functools.partial(
            factor_kernel, n_own=len(own), total_rows=total_rows, apply=applied is not None
        ),
        name="factor" if applied is None else "factor_apply",
        out_shape=out_shape,
        in_specs=[pl.BlockSpec(memory_space=pltpu.SMEM)] + [vmem] * len(args),
        out_specs=vmem,
        scratch_shapes=[pltpu.VMEM((nv, nv), f32), pltpu.VMEM((nv, nv), f32)],
    )(parity, *args)


def local(blocks, coords, vectors):
    n_row = lax.axis_size("row")
    n_col = lax.axis_size("col")
    group = vectors.shape[1]
    total_rows = 2 * group * n_row * n_col
    values = blocks.reshape(blocks.shape[2], blocks.shape[3], blocks.shape[4])
    places = coords.reshape(2, coords.shape[3])
    row_id = lax.axis_index("row")
    col_id = lax.axis_index("col")
    here_direct = jnp.stack([row_id, col_id]).astype(jnp.int32)
    here_flipped = jnp.stack([col_id, row_id]).astype(jnp.int32)
    parity = (col_id & 1).astype(jnp.int32).reshape(1)
    even = list(range(2, n_col, 2))
    row_masks = list(range(1, n_row))

    def spread_row(x):
        return [x] + [swap(x, "row", m) for m in row_masks]

    def spread_col(x):
        far = [swap(x, "col", m) for m in even]
        near = swap(x, "col", 1)
        joined = [swap(f, "col", 1) for f in far]
        return [x, near] + far + joined

    row_shards = [[0]] + [[m] for m in row_masks]
    col_shards = [[0], [1]] + [[m] for m in even] + [[m ^ 1] for m in even]
    col_out = [[0] + even, [m ^ 1 for m in [0] + even]]

    def direct(pieces):
        return tile_products(values, places, here_direct, pieces, row_shards, col_out, False)

    def flipped(pieces):
        return tile_products(values, places, here_flipped, pieces, col_shards, row_shards, True)

    def gather_col(outs):
        mine, others = outs
        both = mine + swap(others, "col", 1)
        parts = [both[i * group : (i + 1) * group] for i in range(len(even) + 1)]
        return [parts[0]] + [swap(p, "col", m) for p, m in zip(parts[1:], even)]

    def gather_row(outs):
        return [outs[0]] + [swap(p, "row", m) for p, m in zip(outs[1:], row_masks)]

    def reduce_gram(mine, other):
        own = mine + swap(other, "col", 1)
        own = functools.reduce(jnp.add, [own] + [swap(own, "col", m) for m in even])
        parts = [own] + [swap(own, "row", m) for m in row_masks]
        own = functools.reduce(jnp.add, parts)
        return [own], swap(own, "col", 1)

    upper, lower = vectors[0], vectors[1]
    pieces_z = spread_row(lower)
    lower1 = functools.reduce(jnp.add, gather_row(flipped(spread_col(upper))))
    upper1 = functools.reduce(jnp.add, gather_col(direct(pieces_z)))
    pieces_z = spread_row(lower1)
    lowers = gather_row(flipped(spread_col(upper1)))
    parts = gram_parts(parity, [upper1], [lower1])
    parts = reduce_gram(*parts)
    weight = factor_inverse(parity, *parts, total_rows)
    uppers = gather_col(direct(pieces_z))
    applied, mine, other = gram_parts(parity, uppers, lowers, weight)
    parts = reduce_gram(mine, other)
    return factor_inverse(parity, *parts, total_rows, applied)


def solution(mesh):
    return jax.shard_map(
        local,
        mesh=mesh,
        in_specs=(
            P("row", "col", None, None, None),
            P("row", "col", None, None),
            P(None, ("row", "col"), None),
        ),
        out_specs=P(None, ("row", "col"), None),
        check_vma=False,
    )
```

```python
import functools

import jax
import jax.numpy as jnp
from jax import lax
from jax.experimental import pallas as pl
from jax.experimental.pallas import tpu as pltpu
from jax.sharding import PartitionSpec as P


f32 = jnp.float32
bf16 = jnp.bfloat16
exact_mode = lax.Precision.HIGHEST


def halves(x):
    hi = x.astype(bf16)
    return hi, (x - hi.astype(f32)).astype(bf16)


def swap(x, axis, mask):
    size = lax.axis_size(axis)
    return lax.ppermute(x, axis, [(i, i ^ mask) for i in range(size)])


def chunk_of(listed):
    for size in range(min(listed, 34), 0, -1):
        if listed % size == 0:
            return size
    return 1


def room(*arrays):
    return sum(a.size * a.dtype.itemsize for a in arrays) + (4 << 20)


def tile_kernel(
    places, here, values_ref, *rest, flipped, in_shards, out_shards, step_blocks, group_blocks
):
    n_in = len(in_shards)
    n_out = len(out_shards)
    in_refs = rest[:n_in]
    out_refs = rest[n_in : n_in + n_out]
    stacked, acc, held, sems = rest[n_in + n_out :]
    listed, blk, _ = values_ref.shape
    steps = listed // step_blocks

    def fetch(step):
        part = pl.ds(step * step_blocks, step_blocks)
        return pltpu.make_async_copy(values_ref.at[part], held.at[part], sems.at[step])

    for step in range(steps):
        fetch(step).start()
    acc[...] = jnp.zeros_like(acc)
    for mask in sorted(set(in_shards)):
        refs = [r for r, m in zip(in_refs, in_shards) if m == mask]
        first = (here[0] ^ mask) * group_blocks
        for g in range(group_blocks):
            part = functools.reduce(jnp.add, [r[pl.ds(g * blk, blk), :] for r in refs])
            both = jnp.concatenate(halves(part), axis=1)
            stacked[first + g, 0:blk, :] = both
            stacked[first + g, blk : 2 * blk, :] = both

    def run(step, carry):
        fetch(step).wait()
        sums = []
        for q in range(step_blocks):
            k = step * step_blocks + q
            i = places[0, k]
            j = places[1, k]
            source, target = (i, j) if flipped else (j, i)
            entry = held[k]
            hi, lo = halves(entry.T if flipped else entry)
            p = jnp.dot(
                jnp.concatenate([hi, lo], axis=1), stacked[source], preferred_element_type=f32
            )
            nv = p.shape[1] // 2
            sums.append((target, p[:, :nv] + p[:, nv:]))
        for target, p in sums:
            acc[target] = acc[target] + p
        return carry

    lax.fori_loop(0, steps, run, 0)
    for ref, shards in zip(out_refs, out_shards):
        for place, mask in enumerate(shards):
            first = (here[1] ^ mask) * group_blocks
            for g in range(group_blocks):
                ref[pl.ds((place * group_blocks + g) * blk, blk), :] = acc[first + g]


def tile_products(values, places, here, pieces, in_shards, out_shards, flipped):
    listed, blk, _ = values.shape
    nv = pieces[0].shape[1]
    group = pieces[0].shape[0]
    group_blocks = group // blk
    step_blocks = chunk_of(listed)
    n_in = len(set(in_shards)) * group_blocks
    n_out = sum(len(s) for s in out_shards) * group_blocks
    vmem = pl.BlockSpec(memory_space=pltpu.VMEM)
    smem = pl.BlockSpec(memory_space=pltpu.SMEM)
    out_shape = [jax.ShapeDtypeStruct((len(s) * group, nv), f32) for s in out_shards]
    scratch = [
        jax.ShapeDtypeStruct((n_in, 2 * blk, 2 * nv), bf16),
        jax.ShapeDtypeStruct((n_out, blk, nv), f32),
        jax.ShapeDtypeStruct(values.shape, f32),
    ]
    body = functools.partial(
        tile_kernel,
        flipped=flipped,
        in_shards=in_shards,
        out_shards=out_shards,
        step_blocks=step_blocks,
        group_blocks=group_blocks,
    )
    return pl.pallas_call(
        body,
        name="tile_flipped" if flipped else "tile_direct",
        out_shape=out_shape,
        in_specs=[smem, smem, pl.BlockSpec(memory_space=pl.ANY)] + [vmem] * len(pieces),
        out_specs=[vmem] * len(out_shape),
        scratch_shapes=[pltpu.VMEM(s.shape, s.dtype) for s in scratch]
        + [pltpu.SemaphoreType.DMA((listed // step_blocks,))],
        compiler_params=pltpu.CompilerParams(vmem_limit_bytes=50 << 20),
        cost_estimate=pl.CostEstimate(
            flops=2 * listed * blk * blk * nv * 4, transcendentals=0, bytes_accessed=values.size * 4
        ),
    )(places, here, values, *pieces)


def gram_kernel(here, *rest, n_upper, n_lower, scale):
    upper_refs = rest[:n_upper]
    lower_refs = rest[n_upper : n_upper + n_lower]
    rest = rest[n_upper + n_lower :]
    if scale:
        w_ref, y_ref, mine_ref, other_ref, full = rest
    else:
        mine_ref, other_ref, full = rest
    total = None
    for band, refs in enumerate((upper_refs, lower_refs)):
        y = refs[0][...]
        for r in refs[1:]:
            y = y + r[...]
        if scale:
            y = jnp.dot(y, w_ref[...], precision=exact_mode, preferred_element_type=f32)
            y_ref[band] = y
        part = lax.dot_general(
            y, y, (((0,), (0,)), ((), ())), precision=exact_mode, preferred_element_type=f32
        )
        total = part if total is None else total + part
    full[...] = total
    half = total.shape[0] // 2
    mine_ref[...] = full[pl.ds(here[0] * half, half), :]
    other_ref[...] = full[pl.ds((1 - here[0]) * half, half), :]


def gram_parts(parity, uppers, lowers, weight=None):
    rows, nv = uppers[0].shape
    half = jax.ShapeDtypeStruct((nv // 2, nv), f32)
    out_shape = [half, half]
    args = list(uppers) + list(lowers)
    if weight is not None:
        out_shape = [jax.ShapeDtypeStruct((2, rows, nv), f32)] + out_shape
        args.append(weight)
    vmem = pl.BlockSpec(memory_space=pltpu.VMEM)
    return pl.pallas_call(
        functools.partial(
            gram_kernel, n_upper=len(uppers), n_lower=len(lowers), scale=weight is not None
        ),
        name="gram_scaled" if weight is not None else "gram_plain",
        out_shape=out_shape,
        in_specs=[pl.BlockSpec(memory_space=pltpu.SMEM)] + [vmem] * len(args),
        out_specs=[vmem] * len(out_shape),
        scratch_shapes=[pltpu.VMEM((nv, nv), f32)],
        compiler_params=pltpu.CompilerParams(vmem_limit_bytes=room(*out_shape, *args)),
    )(parity, *args)


def factor_kernel(here, *rest, n_own, total_rows, apply):
    own_refs = rest[:n_own]
    other_ref = rest[n_own]
    rest = rest[n_own + 1 :]
    if apply:
        y_ref, out_ref, full, rows = rest
    else:
        w_ref, full, rows = rest
    size = full.shape[0]
    half = size // 2
    own = own_refs[0][...]
    for r in own_refs[1:]:
        own = own + r[...]
    full[pl.ds(here[0] * half, half), :] = own
    full[pl.ds((1 - here[0]) * half, half), :] = other_ref[...]
    sub = 8
    groups = size // sub
    lane = lax.broadcasted_iota(jnp.int32, (sub, size), 1)
    row_in = lax.broadcasted_iota(jnp.int32, (sub, size), 0)

    def spread(x, k):
        return jnp.broadcast_to(x[:, k : k + 1], (sub, size))

    m = [full[pl.ds(g * sub, sub), :] for g in range(groups)]
    kept = [jnp.where(lane == row_in + g * sub, m[g], 0.0) for g in range(groups)]
    across = functools.reduce(jnp.add, [jnp.sum(x, axis=0, keepdims=True) for x in kept])
    inv_rows = 1.0 / total_rows
    unit_row = lax.rsqrt(across * inv_rows)
    for g in range(groups):
        unit_col = lax.rsqrt(jnp.sum(kept[g], axis=1, keepdims=True) * inv_rows)
        m[g] = (m[g] * inv_rows * unit_row) * unit_col

    for g0 in range(groups):
        k = g0 * sub
        rows[pl.ds(k, sub), :] = m[g0]
        r = [rows[pl.ds(k + i, sub, stride=0), :] for i in range(sub)]
        s = {(i, j): spread(r[i], k + j) for i in range(sub) for j in range(i, sub)}
        in_panel = (lane >= k) & (lane < k + sub)
        done = lane < k + sub
        r = [jnp.where(lane == k + i, 1.0, jnp.where(in_panel, 0.0, r[i])) for i in range(sub)]
        f = [None] * sub
        q = {}
        for i in range(0, sub, 2):
            a, b, c = s[i, i], s[i, i + 1], s[i + 1, i + 1]
            inv = 1.0 / (a * c - b * b)
            t = b / a
            first = jnp.where(done, r[i], 0.0) * lax.rsqrt(a)
            second = jnp.where(done, r[i + 1] - t * r[i], 0.0) * lax.rsqrt(c - b * t)
            full[pl.ds(k + i, 1), :] = first[0:1]
            full[pl.ds(k + i + 1, 1), :] = second[0:1]
            a, b, c = a * inv, b * inv, c * inv
            f[i] = c * r[i] - b * r[i + 1]
            f[i + 1] = a * r[i + 1] - b * r[i]
            for j in range(i + 2, sub):
                q[i, j] = c * s[i, j] - b * s[i + 1, j]
                q[i + 1, j] = a * s[i + 1, j] - b * s[i, j]
            for j in range(i + 2, sub):
                r[j] = r[j] - (s[i, j] * f[i] + s[i + 1, j] * f[i + 1])
                for l in range(j, sub):
                    s[j, l] = s[j, l] - (s[i, j] * q[i, l] + s[i + 1, j] * q[i + 1, l])
        for i in range(sub - 4, -1, -2):
            for j in range(i + 2, sub):
                f[i] = f[i] - q[i, j] * f[j]
                f[i + 1] = f[i + 1] - q[i + 1, j] * f[j]
        for g in range(g0 + 1, groups):
            change = spread(m[g], k) * f[0]
            for j in range(1, sub):
                change = change + spread(m[g], k + j) * f[j]
            m[g] = jnp.where(in_panel, 0.0, m[g]) - change

    inverse = full[...] * unit_row
    if apply:
        for band in range(2):
            out_ref[band] = lax.dot_general(
                y_ref[band],
                inverse,
                (((1,), (1,)), ((), ())),
                precision=exact_mode,
                preferred_element_type=f32,
            )
    else:
        w_ref[...] = inverse.T


def factor_inverse(parity, own, other, total_rows, applied=None):
    _, nv = other.shape
    vmem = pl.BlockSpec(memory_space=pltpu.VMEM)
    args = list(own) + [other]
    if applied is None:
        out_shape = jax.ShapeDtypeStruct((nv, nv), f32)
    else:
        out_shape = jax.ShapeDtypeStruct(applied.shape, f32)
        args.append(applied)
    return pl.pallas_call(
        functools.partial(
            factor_kernel, n_own=len(own), total_rows=total_rows, apply=applied is not None
        ),
        name="factor" if applied is None else "factor_apply",
        out_shape=out_shape,
        in_specs=[pl.BlockSpec(memory_space=pltpu.SMEM)] + [vmem] * len(args),
        out_specs=vmem,
        scratch_shapes=[pltpu.VMEM((nv, nv), f32), pltpu.VMEM((nv, nv), f32)],
        compiler_params=pltpu.CompilerParams(vmem_limit_bytes=room(out_shape, *args)),
    )(parity, *args)


def local(blocks, coords, vectors):
    n_row = lax.axis_size("row")
    n_col = lax.axis_size("col")
    group = vectors.shape[1]
    total_rows = 2 * group * n_row * n_col
    values = blocks.reshape(blocks.shape[2], blocks.shape[3], blocks.shape[4])
    places = coords.reshape(2, coords.shape[3])
    row_id = lax.axis_index("row")
    col_id = lax.axis_index("col")
    here_direct = jnp.stack([row_id, col_id]).astype(jnp.int32)
    here_flipped = jnp.stack([col_id, row_id]).astype(jnp.int32)
    parity = (col_id & 1).astype(jnp.int32).reshape(1)
    even = list(range(2, n_col, 2))
    row_masks = list(range(1, n_row))

    def spread_row(x):
        if n_row != 4:
            return [x] + [swap(x, "row", m) for m in row_masks]
        two = swap(x, "row", 2)
        one = swap(x, "row", 1)
        inner = lax.ppermute(x, "row", [(1, 2), (2, 1)])
        outer = lax.ppermute(two, "row", [(1, 0), (2, 3)])
        return [x, one, two, inner, outer]

    def spread_col(x):
        far = [swap(x, "col", m) for m in even]
        near = swap(x, "col", 1)
        joined = [swap(f, "col", 1) for f in far]
        return [x, near] + far + joined

    row_in = [0] + row_masks + ([3] if n_row == 4 else [])
    row_out = [[m] for m in [0] + row_masks]
    col_in = [0, 1] + even + [m ^ 1 for m in even]
    col_out = [[0] + even, [m ^ 1 for m in [0] + even]]

    def direct(pieces):
        return tile_products(values, places, here_direct, pieces, row_in, col_out, False)

    def flipped(pieces):
        return tile_products(values, places, here_flipped, pieces, col_in, row_out, True)

    def gather_col(outs):
        mine, others = outs
        both = mine + swap(others, "col", 1)
        parts = [both[i * group : (i + 1) * group] for i in range(len(even) + 1)]
        return [parts[0]] + [swap(p, "col", m) for p, m in zip(parts[1:], even)]

    def gather_row(outs):
        return [outs[0]] + [swap(p, "row", m) for p, m in zip(outs[1:], row_masks)]

    def reduce_gram(mine, other):
        own = mine + swap(other, "col", 1)
        own = functools.reduce(jnp.add, [own] + [swap(own, "col", m) for m in even])
        parts = [own] + [swap(own, "row", m) for m in row_masks]
        own = functools.reduce(jnp.add, parts)
        return [own], swap(own, "col", 1)

    upper, lower = vectors[0], vectors[1]
    pieces_z = spread_row(lower)
    lower1 = functools.reduce(jnp.add, gather_row(flipped(spread_col(upper))))
    upper1 = functools.reduce(jnp.add, gather_col(direct(pieces_z)))
    pieces_z = spread_row(lower1)
    lowers = gather_row(flipped(spread_col(upper1)))
    parts = gram_parts(parity, [upper1], [lower1])
    parts = reduce_gram(*parts)
    weight = factor_inverse(parity, *parts, total_rows)
    uppers = gather_col(direct(pieces_z))
    applied, mine, other = gram_parts(parity, uppers, lowers, weight)
    parts = reduce_gram(mine, other)
    return factor_inverse(parity, *parts, total_rows, applied)


def solution(mesh):
    return jax.shard_map(
        local,
        mesh=mesh,
        in_specs=(
            P("row", "col", None, None, None),
            P("row", "col", None, None),
            P(None, ("row", "col"), None),
        ),
        out_specs=P(None, ("row", "col"), None),
        check_vma=False,
    )
```

```python
import functools

import jax
import jax.numpy as jnp
from jax import lax
from jax.experimental import pallas as pl
from jax.experimental.pallas import tpu as pltpu
from jax.sharding import PartitionSpec as P


f32 = jnp.float32
bf16 = jnp.bfloat16
exact_mode = lax.Precision.HIGHEST


def halves(x):
    hi = x.astype(bf16)
    return hi, (x - hi.astype(f32)).astype(bf16)


def swap(x, axis, mask):
    size = lax.axis_size(axis)
    return lax.ppermute(x, axis, [(i, i ^ mask) for i in range(size)])


def chunk_of(listed):
    for size in range(min(listed, 34), 0, -1):
        if listed % size == 0:
            return size
    return 1


def room(*arrays):
    return sum(a.size * a.dtype.itemsize for a in arrays) + (4 << 20)


def tile_kernel(
    places, here, values_ref, *rest, flipped, in_shards, out_shards, step_blocks, group_blocks
):
    n_in = len(in_shards)
    n_out = len(out_shards)
    in_refs = rest[:n_in]
    out_refs = rest[n_in : n_in + n_out]
    stacked, acc, held, sems = rest[n_in + n_out :]
    listed, blk, _ = values_ref.shape
    steps = listed // step_blocks

    def fetch(step):
        part = pl.ds(step * step_blocks, step_blocks)
        return pltpu.make_async_copy(values_ref.at[part], held.at[part], sems.at[step])

    for step in range(steps):
        fetch(step).start()
    acc[...] = jnp.zeros_like(acc)
    for mask in sorted(set(in_shards)):
        refs = [r for r, m in zip(in_refs, in_shards) if m == mask]
        first = (here[0] ^ mask) * group_blocks
        for g in range(group_blocks):
            part = functools.reduce(jnp.add, [r[pl.ds(g * blk, blk), :] for r in refs])
            both = jnp.concatenate(halves(part), axis=1)
            stacked[first + g, 0:blk, :] = both
            stacked[first + g, blk : 2 * blk, :] = both

    def run(step, carry):
        fetch(step).wait()
        sums = []
        for q in range(step_blocks):
            k = step * step_blocks + q
            i = places[0, k]
            j = places[1, k]
            source, target = (i, j) if flipped else (j, i)
            entry = held[k]
            hi, lo = halves(entry.T if flipped else entry)
            p = jnp.dot(
                jnp.concatenate([hi, lo], axis=1), stacked[source], preferred_element_type=f32
            )
            nv = p.shape[1] // 2
            sums.append((target, p[:, :nv] + p[:, nv:]))
        for target, p in sums:
            acc[target] = acc[target] + p
        return carry

    lax.fori_loop(0, steps, run, 0)
    for ref, shards in zip(out_refs, out_shards):
        for place, mask in enumerate(shards):
            first = (here[1] ^ mask) * group_blocks
            for g in range(group_blocks):
                ref[pl.ds((place * group_blocks + g) * blk, blk), :] = acc[first + g]


def tile_products(values, places, here, pieces, in_shards, out_shards, flipped):
    listed, blk, _ = values.shape
    nv = pieces[0].shape[1]
    group = pieces[0].shape[0]
    group_blocks = group // blk
    step_blocks = chunk_of(listed)
    n_in = len(set(in_shards)) * group_blocks
    n_out = sum(len(s) for s in out_shards) * group_blocks
    vmem = pl.BlockSpec(memory_space=pltpu.VMEM)
    smem = pl.BlockSpec(memory_space=pltpu.SMEM)
    out_shape = [jax.ShapeDtypeStruct((len(s) * group, nv), f32) for s in out_shards]
    scratch = [
        jax.ShapeDtypeStruct((n_in, 2 * blk, 2 * nv), bf16),
        jax.ShapeDtypeStruct((n_out, blk, nv), f32),
        jax.ShapeDtypeStruct(values.shape, f32),
    ]
    body = functools.partial(
        tile_kernel,
        flipped=flipped,
        in_shards=in_shards,
        out_shards=out_shards,
        step_blocks=step_blocks,
        group_blocks=group_blocks,
    )
    return pl.pallas_call(
        body,
        name="tile_flipped" if flipped else "tile_direct",
        out_shape=out_shape,
        in_specs=[smem, smem, pl.BlockSpec(memory_space=pl.ANY)] + [vmem] * len(pieces),
        out_specs=[vmem] * len(out_shape),
        scratch_shapes=[pltpu.VMEM(s.shape, s.dtype) for s in scratch]
        + [pltpu.SemaphoreType.DMA((listed // step_blocks,))],
        compiler_params=pltpu.CompilerParams(vmem_limit_bytes=50 << 20),
        cost_estimate=pl.CostEstimate(
            flops=2 * listed * blk * blk * nv * 4, transcendentals=0, bytes_accessed=values.size * 4
        ),
    )(places, here, values, *pieces)


def gram_kernel(here, *rest, n_upper, n_lower, scale):
    upper_refs = rest[:n_upper]
    lower_refs = rest[n_upper : n_upper + n_lower]
    rest = rest[n_upper + n_lower :]
    if scale:
        w_ref, y_ref, mine_ref, other_ref, full = rest
    else:
        mine_ref, other_ref, full = rest
    total = None
    for band, refs in enumerate((upper_refs, lower_refs)):
        y = refs[0][...]
        for r in refs[1:]:
            y = y + r[...]
        if scale:
            y = jnp.dot(y, w_ref[...], precision=exact_mode, preferred_element_type=f32)
            y_ref[band] = y
        part = lax.dot_general(
            y, y, (((0,), (0,)), ((), ())), precision=exact_mode, preferred_element_type=f32
        )
        total = part if total is None else total + part
    full[...] = total
    half = total.shape[0] // 2
    mine_ref[...] = full[pl.ds(here[0] * half, half), :]
    other_ref[...] = full[pl.ds((1 - here[0]) * half, half), :]


def gram_parts(parity, uppers, lowers, weight=None):
    rows, nv = uppers[0].shape
    half = jax.ShapeDtypeStruct((nv // 2, nv), f32)
    out_shape = [half, half]
    args = list(uppers) + list(lowers)
    if weight is not None:
        out_shape = [jax.ShapeDtypeStruct((2, rows, nv), f32)] + out_shape
        args.append(weight)
    vmem = pl.BlockSpec(memory_space=pltpu.VMEM)
    return pl.pallas_call(
        functools.partial(
            gram_kernel, n_upper=len(uppers), n_lower=len(lowers), scale=weight is not None
        ),
        name="gram_scaled" if weight is not None else "gram_plain",
        out_shape=out_shape,
        in_specs=[pl.BlockSpec(memory_space=pltpu.SMEM)] + [vmem] * len(args),
        out_specs=[vmem] * len(out_shape),
        scratch_shapes=[pltpu.VMEM((nv, nv), f32)],
        compiler_params=pltpu.CompilerParams(vmem_limit_bytes=room(*out_shape, *args)),
    )(parity, *args)


def factor_kernel(here, *rest, n_own, total_rows, apply):
    own_refs = rest[:n_own]
    other_ref = rest[n_own]
    rest = rest[n_own + 1 :]
    if apply:
        y_ref, out_ref, full, rows = rest
    else:
        w_ref, full, rows = rest
    size = full.shape[0]
    half = size // 2
    own = own_refs[0][...]
    for r in own_refs[1:]:
        own = own + r[...]
    full[pl.ds(here[0] * half, half), :] = own
    full[pl.ds((1 - here[0]) * half, half), :] = other_ref[...]
    sub = 8
    groups = size // sub
    lane = lax.broadcasted_iota(jnp.int32, (sub, size), 1)
    row_in = lax.broadcasted_iota(jnp.int32, (sub, size), 0)

    def spread(x, k):
        return jnp.broadcast_to(x[:, k : k + 1], (sub, size))

    m = [full[pl.ds(g * sub, sub), :] for g in range(groups)]
    kept = [jnp.where(lane == row_in + g * sub, m[g], 0.0) for g in range(groups)]
    across = functools.reduce(jnp.add, [jnp.sum(x, axis=0, keepdims=True) for x in kept])
    inv_rows = 1.0 / total_rows
    unit_row = lax.rsqrt(across * inv_rows)
    for g in range(groups):
        unit_col = lax.rsqrt(jnp.sum(kept[g], axis=1, keepdims=True) * inv_rows)
        m[g] = (m[g] * inv_rows * unit_row) * unit_col

    for g0 in range(groups):
        k = g0 * sub
        rows[pl.ds(k, sub), :] = m[g0]
        r = [rows[pl.ds(k + i, sub, stride=0), :] for i in range(sub)]
        s = {(i, j): spread(r[i], k + j) for i in range(sub) for j in range(i, sub)}
        in_panel = (lane >= k) & (lane < k + sub)
        done = lane < k + sub
        r = [jnp.where(lane == k + i, 1.0, jnp.where(in_panel, 0.0, r[i])) for i in range(sub)]
        f = [None] * sub
        q = {}
        for i in range(0, sub, 2):
            a, b, c = s[i, i], s[i, i + 1], s[i + 1, i + 1]
            inv = 1.0 / (a * c - b * b)
            t = b / a
            first = jnp.where(done, r[i], 0.0) * lax.rsqrt(a)
            second = jnp.where(done, r[i + 1] - t * r[i], 0.0) * lax.rsqrt(c - b * t)
            full[pl.ds(k + i, 1), :] = first[0:1]
            full[pl.ds(k + i + 1, 1), :] = second[0:1]
            a, b, c = a * inv, b * inv, c * inv
            f[i] = c * r[i] - b * r[i + 1]
            f[i + 1] = a * r[i + 1] - b * r[i]
            for j in range(i + 2, sub):
                q[i, j] = c * s[i, j] - b * s[i + 1, j]
                q[i + 1, j] = a * s[i + 1, j] - b * s[i, j]
            for j in range(i + 2, sub):
                r[j] = r[j] - (s[i, j] * f[i] + s[i + 1, j] * f[i + 1])
                for l in range(j, sub):
                    s[j, l] = s[j, l] - (s[i, j] * q[i, l] + s[i + 1, j] * q[i + 1, l])
        for i in range(sub - 4, -1, -2):
            for j in range(i + 2, sub):
                f[i] = f[i] - q[i, j] * f[j]
                f[i + 1] = f[i + 1] - q[i + 1, j] * f[j]
        for g in range(g0 + 1, groups):
            change = spread(m[g], k) * f[0]
            for j in range(1, sub):
                change = change + spread(m[g], k + j) * f[j]
            m[g] = jnp.where(in_panel, 0.0, m[g]) - change

    inverse = full[...] * unit_row
    if apply:
        for band in range(2):
            out_ref[band] = lax.dot_general(
                y_ref[band],
                inverse,
                (((1,), (1,)), ((), ())),
                precision=exact_mode,
                preferred_element_type=f32,
            )
    else:
        w_ref[...] = inverse.T


def factor_inverse(parity, own, other, total_rows, applied=None):
    _, nv = other.shape
    vmem = pl.BlockSpec(memory_space=pltpu.VMEM)
    args = list(own) + [other]
    if applied is None:
        out_shape = jax.ShapeDtypeStruct((nv, nv), f32)
    else:
        out_shape = jax.ShapeDtypeStruct(applied.shape, f32)
        args.append(applied)
    return pl.pallas_call(
        functools.partial(
            factor_kernel, n_own=len(own), total_rows=total_rows, apply=applied is not None
        ),
        name="factor" if applied is None else "factor_apply",
        out_shape=out_shape,
        in_specs=[pl.BlockSpec(memory_space=pltpu.SMEM)] + [vmem] * len(args),
        out_specs=vmem,
        scratch_shapes=[pltpu.VMEM((nv, nv), f32), pltpu.VMEM((nv, nv), f32)],
        compiler_params=pltpu.CompilerParams(vmem_limit_bytes=room(out_shape, *args)),
    )(parity, *args)


def local(blocks, coords, vectors):
    n_row = lax.axis_size("row")
    n_col = lax.axis_size("col")
    group = vectors.shape[1]
    total_rows = 2 * group * n_row * n_col
    values = blocks.reshape(blocks.shape[2], blocks.shape[3], blocks.shape[4])
    places = coords.reshape(2, coords.shape[3])
    row_id = lax.axis_index("row")
    col_id = lax.axis_index("col")
    here_direct = jnp.stack([row_id, col_id]).astype(jnp.int32)
    here_flipped = jnp.stack([col_id, row_id]).astype(jnp.int32)
    parity = (col_id & 1).astype(jnp.int32).reshape(1)
    even = list(range(2, n_col, 2))
    row_masks = list(range(1, n_row))[::-1]

    def spread_row(x):
        if n_row != 4:
            return [x] + [swap(x, "row", m) for m in row_masks]
        two = swap(x, "row", 2)
        one = swap(x, "row", 1)
        inner = lax.ppermute(x, "row", [(1, 2), (2, 1)])
        outer = lax.ppermute(two, "row", [(1, 0), (2, 3)])
        return [x, one, two, inner, outer]

    def spread_col(x):
        far = [swap(x, "col", m) for m in even]
        near = swap(x, "col", 1)
        joined = [swap(f, "col", 1) for f in far]
        return [x, near] + far + joined

    row_in = [0, 1, 2, 3, 3] if n_row == 4 else [0] + row_masks
    row_out = [[m] for m in [0] + row_masks]
    col_in = [0, 1] + even + [m ^ 1 for m in even]
    order = even + [0]
    col_masks = [p for p in (order[: len(order) // 2], order[len(order) // 2 :]) if p]
    col_out = col_masks + [[m ^ 1 for m in p] for p in col_masks]

    def direct(pieces):
        return tile_products(values, places, here_direct, pieces, row_in, col_out, False)

    def flipped(pieces):
        return tile_products(values, places, here_flipped, pieces, col_in, row_out, True)

    def gather_col(outs):
        count = len(col_masks)
        parts = []
        for mine, others, masks in zip(outs[:count], outs[count:], col_masks):
            both = mine + swap(others, "col", 1)
            parts += [both[i * group : (i + 1) * group] for i in range(len(masks))]
        return [parts[-1]] + [swap(p, "col", m) for p, m in zip(parts, even)]

    def gather_row(outs):
        return [outs[0]] + [swap(p, "row", m) for p, m in zip(outs[1:], row_masks)]

    def reduce_gram(mine, other):
        own = mine + swap(other, "col", 1)
        own = functools.reduce(jnp.add, [own] + [swap(own, "col", m) for m in even])
        parts = [own] + [swap(own, "row", m) for m in row_masks]
        own = functools.reduce(jnp.add, parts)
        return [own], swap(own, "col", 1)

    upper, lower = vectors[0], vectors[1]
    pieces_z = spread_row(lower)
    lower1 = functools.reduce(jnp.add, gather_row(flipped(spread_col(upper))))
    upper1 = functools.reduce(jnp.add, gather_col(direct(pieces_z)))
    pieces_z = spread_row(lower1)
    lowers = gather_row(flipped(spread_col(upper1)))
    parts = gram_parts(parity, [upper1], [lower1])
    parts = reduce_gram(*parts)
    weight = factor_inverse(parity, *parts, total_rows)
    uppers = gather_col(direct(pieces_z))
    applied, mine, other = gram_parts(parity, uppers, lowers, weight)
    parts = reduce_gram(mine, other)
    return factor_inverse(parity, *parts, total_rows, applied)


def solution(mesh):
    return jax.shard_map(
        local,
        mesh=mesh,
        in_specs=(
            P("row", "col", None, None, None),
            P("row", "col", None, None),
            P(None, ("row", "col"), None),
        ),
        out_specs=P(None, ("row", "col"), None),
        check_vma=False,
    )
```

```python
import functools

import jax
import jax.numpy as jnp
from jax import lax
from jax.experimental import pallas as pl
from jax.experimental.pallas import tpu as pltpu
from jax.sharding import PartitionSpec as P


f32 = jnp.float32
bf16 = jnp.bfloat16
exact_mode = lax.Precision.HIGHEST


def halves(x):
    hi = x.astype(bf16)
    return hi, (x - hi.astype(f32)).astype(bf16)


def swap(x, axis, mask):
    size = lax.axis_size(axis)
    return lax.ppermute(x, axis, [(i, i ^ mask) for i in range(size)])


def chunk_of(listed):
    for size in range(min(listed, 34), 0, -1):
        if listed % size == 0:
            return size
    return 1


def room(*arrays):
    return sum(a.size * a.dtype.itemsize for a in arrays) + (4 << 20)


def tile_kernel(
    places, here, values_ref, *rest, flipped, in_shards, out_shards, step_blocks, group_blocks
):
    n_in = len(in_shards)
    n_out = len(out_shards)
    in_refs = rest[:n_in]
    out_refs = rest[n_in : n_in + n_out]
    stacked, acc, held, sems = rest[n_in + n_out :]
    listed, blk, _ = values_ref.shape
    steps = listed // step_blocks

    def fetch(step):
        part = pl.ds(step * step_blocks, step_blocks)
        return pltpu.make_async_copy(values_ref.at[part], held.at[part], sems.at[step])

    for step in range(steps):
        fetch(step).start()
    acc[...] = jnp.zeros_like(acc)
    for mask in sorted(set(in_shards)):
        refs = [r for r, m in zip(in_refs, in_shards) if m == mask]
        first = (here[0] ^ mask) * group_blocks
        for g in range(group_blocks):
            part = functools.reduce(jnp.add, [r[pl.ds(g * blk, blk), :] for r in refs])
            both = jnp.concatenate(halves(part), axis=1)
            stacked[first + g, 0:blk, :] = both
            stacked[first + g, blk : 2 * blk, :] = both

    def run(step, carry):
        fetch(step).wait()
        sums = []
        for q in range(step_blocks):
            k = step * step_blocks + q
            i = places[0, k]
            j = places[1, k]
            source, target = (i, j) if flipped else (j, i)
            entry = held[k]
            hi, lo = halves(entry.T if flipped else entry)
            p = jnp.dot(
                jnp.concatenate([hi, lo], axis=1), stacked[source], preferred_element_type=f32
            )
            nv = p.shape[1] // 2
            sums.append((target, p[:, :nv] + p[:, nv:]))
        for target, p in sums:
            acc[target] = acc[target] + p
        return carry

    lax.fori_loop(0, steps, run, 0)
    for ref, shards in zip(out_refs, out_shards):
        for place, mask in enumerate(shards):
            first = (here[1] ^ mask) * group_blocks
            for g in range(group_blocks):
                ref[pl.ds((place * group_blocks + g) * blk, blk), :] = acc[first + g]


def tile_products(values, places, here, pieces, in_shards, out_shards, flipped):
    listed, blk, _ = values.shape
    nv = pieces[0].shape[1]
    group = pieces[0].shape[0]
    group_blocks = group // blk
    step_blocks = chunk_of(listed)
    n_in = len(set(in_shards)) * group_blocks
    n_out = sum(len(s) for s in out_shards) * group_blocks
    vmem = pl.BlockSpec(memory_space=pltpu.VMEM)
    smem = pl.BlockSpec(memory_space=pltpu.SMEM)
    out_shape = [jax.ShapeDtypeStruct((len(s) * group, nv), f32) for s in out_shards]
    scratch = [
        jax.ShapeDtypeStruct((n_in, 2 * blk, 2 * nv), bf16),
        jax.ShapeDtypeStruct((n_out, blk, nv), f32),
        jax.ShapeDtypeStruct(values.shape, f32),
    ]
    body = functools.partial(
        tile_kernel,
        flipped=flipped,
        in_shards=in_shards,
        out_shards=out_shards,
        step_blocks=step_blocks,
        group_blocks=group_blocks,
    )
    return pl.pallas_call(
        body,
        name="tile_flipped" if flipped else "tile_direct",
        out_shape=out_shape,
        in_specs=[smem, smem, pl.BlockSpec(memory_space=pl.ANY)] + [vmem] * len(pieces),
        out_specs=[vmem] * len(out_shape),
        scratch_shapes=[pltpu.VMEM(s.shape, s.dtype) for s in scratch]
        + [pltpu.SemaphoreType.DMA((listed // step_blocks,))],
        compiler_params=pltpu.CompilerParams(vmem_limit_bytes=50 << 20),
        cost_estimate=pl.CostEstimate(
            flops=2 * listed * blk * blk * nv * 4, transcendentals=0, bytes_accessed=values.size * 4
        ),
    )(places, here, values, *pieces)


def gram_kernel(here, *rest, n_upper, n_lower, scale):
    upper_refs = rest[:n_upper]
    lower_refs = rest[n_upper : n_upper + n_lower]
    rest = rest[n_upper + n_lower :]
    if scale:
        w_ref, y_ref, mine_ref, other_ref, full = rest
    else:
        mine_ref, other_ref, full = rest
    total = None
    for band, refs in enumerate((upper_refs, lower_refs)):
        y = refs[0][...]
        for r in refs[1:]:
            y = y + r[...]
        if scale:
            y = jnp.dot(y, w_ref[...], precision=exact_mode, preferred_element_type=f32)
            y_ref[band] = y
        part = lax.dot_general(
            y, y, (((0,), (0,)), ((), ())), precision=exact_mode, preferred_element_type=f32
        )
        total = part if total is None else total + part
    full[...] = total
    half = total.shape[0] // 2
    mine_ref[...] = full[pl.ds(here[0] * half, half), :]
    other_ref[...] = full[pl.ds((1 - here[0]) * half, half), :]


def gram_parts(parity, uppers, lowers, weight=None):
    rows, nv = uppers[0].shape
    half = jax.ShapeDtypeStruct((nv // 2, nv), f32)
    out_shape = [half, half]
    args = list(uppers) + list(lowers)
    if weight is not None:
        out_shape = [jax.ShapeDtypeStruct((2, rows, nv), f32)] + out_shape
        args.append(weight)
    vmem = pl.BlockSpec(memory_space=pltpu.VMEM)
    return pl.pallas_call(
        functools.partial(
            gram_kernel, n_upper=len(uppers), n_lower=len(lowers), scale=weight is not None
        ),
        name="gram_scaled" if weight is not None else "gram_plain",
        out_shape=out_shape,
        in_specs=[pl.BlockSpec(memory_space=pltpu.SMEM)] + [vmem] * len(args),
        out_specs=[vmem] * len(out_shape),
        scratch_shapes=[pltpu.VMEM((nv, nv), f32)],
        compiler_params=pltpu.CompilerParams(vmem_limit_bytes=room(*out_shape, *args)),
    )(parity, *args)


def factor_kernel(here, *rest, n_own, total_rows, apply):
    own_refs = rest[:n_own]
    other_ref = rest[n_own]
    rest = rest[n_own + 1 :]
    if apply:
        y_ref, out_ref, full, rows = rest
    else:
        w_ref, full, rows = rest
    size = full.shape[0]
    half = size // 2
    own = own_refs[0][...]
    for r in own_refs[1:]:
        own = own + r[...]
    full[pl.ds(here[0] * half, half), :] = own
    full[pl.ds((1 - here[0]) * half, half), :] = other_ref[...]
    sub = 8
    groups = size // sub
    lane = lax.broadcasted_iota(jnp.int32, (sub, size), 1)
    row_in = lax.broadcasted_iota(jnp.int32, (sub, size), 0)

    def spread(x, k):
        return jnp.broadcast_to(x[:, k : k + 1], (sub, size))

    m = [full[pl.ds(g * sub, sub), :] for g in range(groups)]
    kept = [jnp.where(lane == row_in + g * sub, m[g], 0.0) for g in range(groups)]
    across = functools.reduce(jnp.add, [jnp.sum(x, axis=0, keepdims=True) for x in kept])
    inv_rows = 1.0 / total_rows
    unit_row = lax.rsqrt(across * inv_rows)
    for g in range(groups):
        unit_col = lax.rsqrt(jnp.sum(kept[g], axis=1, keepdims=True) * inv_rows)
        m[g] = (m[g] * inv_rows * unit_row) * unit_col

    for g0 in range(groups):
        k = g0 * sub
        rows[pl.ds(k, sub), :] = m[g0]
        r = [rows[pl.ds(k + i, sub, stride=0), :] for i in range(sub)]
        s = {(i, j): spread(r[i], k + j) for i in range(sub) for j in range(i, sub)}
        in_panel = (lane >= k) & (lane < k + sub)
        done = lane < k + sub
        r = [jnp.where(lane == k + i, 1.0, jnp.where(in_panel, 0.0, r[i])) for i in range(sub)]
        f = [None] * sub
        q = {}
        for i in range(0, sub, 2):
            a, b, c = s[i, i], s[i, i + 1], s[i + 1, i + 1]
            inv = 1.0 / (a * c - b * b)
            t = b / a
            first = jnp.where(done, r[i], 0.0) * lax.rsqrt(a)
            second = jnp.where(done, r[i + 1] - t * r[i], 0.0) * lax.rsqrt(c - b * t)
            full[pl.ds(k + i, 1), :] = first[0:1]
            full[pl.ds(k + i + 1, 1), :] = second[0:1]
            a, b, c = a * inv, b * inv, c * inv
            f[i] = c * r[i] - b * r[i + 1]
            f[i + 1] = a * r[i + 1] - b * r[i]
            for j in range(i + 2, sub):
                q[i, j] = c * s[i, j] - b * s[i + 1, j]
                q[i + 1, j] = a * s[i + 1, j] - b * s[i, j]
            for j in range(i + 2, sub):
                r[j] = r[j] - (s[i, j] * f[i] + s[i + 1, j] * f[i + 1])
                for l in range(j, sub):
                    s[j, l] = s[j, l] - (s[i, j] * q[i, l] + s[i + 1, j] * q[i + 1, l])
        for i in range(sub - 4, -1, -2):
            for j in range(i + 2, sub):
                f[i] = f[i] - q[i, j] * f[j]
                f[i + 1] = f[i + 1] - q[i + 1, j] * f[j]
        for g in range(g0 + 1, groups):
            change = spread(m[g], k) * f[0]
            for j in range(1, sub):
                change = change + spread(m[g], k + j) * f[j]
            m[g] = jnp.where(in_panel, 0.0, m[g]) - change

    inverse = full[...] * unit_row
    if apply:
        for band in range(2):
            out_ref[band] = lax.dot_general(
                y_ref[band],
                inverse,
                (((1,), (1,)), ((), ())),
                precision=exact_mode,
                preferred_element_type=f32,
            )
    else:
        w_ref[...] = inverse.T


def factor_inverse(parity, own, other, total_rows, applied=None):
    _, nv = other.shape
    vmem = pl.BlockSpec(memory_space=pltpu.VMEM)
    args = list(own) + [other]
    if applied is None:
        out_shape = jax.ShapeDtypeStruct((nv, nv), f32)
    else:
        out_shape = jax.ShapeDtypeStruct(applied.shape, f32)
        args.append(applied)
    return pl.pallas_call(
        functools.partial(
            factor_kernel, n_own=len(own), total_rows=total_rows, apply=applied is not None
        ),
        name="factor" if applied is None else "factor_apply",
        out_shape=out_shape,
        in_specs=[pl.BlockSpec(memory_space=pltpu.SMEM)] + [vmem] * len(args),
        out_specs=vmem,
        scratch_shapes=[pltpu.VMEM((nv, nv), f32), pltpu.VMEM((nv, nv), f32)],
        compiler_params=pltpu.CompilerParams(vmem_limit_bytes=room(out_shape, *args)),
    )(parity, *args)


def local(blocks, coords, vectors):
    n_row = lax.axis_size("row")
    n_col = lax.axis_size("col")
    group = vectors.shape[1]
    total_rows = 2 * group * n_row * n_col
    values = blocks.reshape(blocks.shape[2], blocks.shape[3], blocks.shape[4])
    places = coords.reshape(2, coords.shape[3])
    row_id = lax.axis_index("row")
    col_id = lax.axis_index("col")
    here_direct = jnp.stack([row_id, col_id]).astype(jnp.int32)
    here_flipped = jnp.stack([col_id, row_id]).astype(jnp.int32)
    parity = (col_id & 1).astype(jnp.int32).reshape(1)
    even = list(range(2, n_col, 2))[::-1]
    row_masks = list(range(1, n_row))[::-1]

    def spread_row(x):
        if n_row != 4:
            return [x] + [swap(x, "row", m) for m in row_masks]
        two = swap(x, "row", 2)
        one = swap(x, "row", 1)
        inner = lax.ppermute(x, "row", [(1, 2), (2, 1)])
        outer = lax.ppermute(two, "row", [(1, 0), (2, 3)])
        return [x, one, two, inner, outer]

    def spread_col(x):
        far = [swap(x, "col", m) for m in even]
        near = swap(x, "col", 1)
        joined = [swap(f, "col", 1) for f in far]
        return [x, near] + far + joined

    row_in = [0, 1, 2, 3, 3] if n_row == 4 else [0] + row_masks
    row_out = [[m] for m in [0] + row_masks]
    col_in = [0, 1] + even + [m ^ 1 for m in even]
    order = even + [0]
    col_masks = [p for p in (order[: len(order) // 2], order[len(order) // 2 :]) if p]
    col_out = col_masks + [[m ^ 1 for m in p] for p in col_masks]

    def direct(pieces):
        return tile_products(values, places, here_direct, pieces, row_in, col_out, False)

    def flipped(pieces):
        return tile_products(values, places, here_flipped, pieces, col_in, row_out, True)

    def gather_col(outs):
        count = len(col_masks)
        parts = []
        for mine, others, masks in zip(outs[:count], outs[count:], col_masks):
            both = mine + swap(others, "col", 1)
            parts += [both[i * group : (i + 1) * group] for i in range(len(masks))]
        return [parts[-1]] + [swap(p, "col", m) for p, m in zip(parts, even)]

    def gather_row(outs):
        got = []
        for p, m in zip(outs[1:], row_masks):
            got.append(swap(p, "row", m))
        return [outs[0]] + got

    def reduce_gram(mine, other):
        own = mine + swap(other, "col", 1)
        own = functools.reduce(jnp.add, [own] + [swap(own, "col", m) for m in even])
        parts = [own] + [swap(own, "row", m) for m in row_masks]
        own = functools.reduce(jnp.add, parts)
        return [own], swap(own, "col", 1)

    upper, lower = vectors[0], vectors[1]
    pieces_z = spread_row(lower)
    lower1 = functools.reduce(jnp.add, gather_row(flipped(spread_col(upper))))
    upper1 = functools.reduce(jnp.add, gather_col(direct(pieces_z)))
    pieces_z = spread_row(lower1)
    lowers = gather_row(flipped(spread_col(upper1)))
    parts = gram_parts(parity, [upper1], [lower1])
    parts = reduce_gram(*parts)
    weight = factor_inverse(parity, *parts, total_rows)
    uppers = gather_col(direct(pieces_z))
    applied, mine, other = gram_parts(parity, uppers, lowers, weight)
    parts = reduce_gram(mine, other)
    return factor_inverse(parity, *parts, total_rows, applied)


def solution(mesh):
    return jax.shard_map(
        local,
        mesh=mesh,
        in_specs=(
            P("row", "col", None, None, None),
            P("row", "col", None, None),
            P(None, ("row", "col"), None),
        ),
        out_specs=P(None, ("row", "col"), None),
        check_vma=False,
    )
```

```python
import functools

import jax
import jax.numpy as jnp
from jax import lax
from jax.experimental import pallas as pl
from jax.experimental.pallas import tpu as pltpu
from jax.sharding import PartitionSpec as P


f32 = jnp.float32
bf16 = jnp.bfloat16
exact_mode = lax.Precision.HIGHEST


def halves(x):
    hi = x.astype(bf16)
    return hi, (x - hi.astype(f32)).astype(bf16)


def swap(x, axis, mask):
    size = lax.axis_size(axis)
    return lax.ppermute(x, axis, [(i, i ^ mask) for i in range(size)])


def chunk_of(listed):
    for size in range(min(listed, 34), 0, -1):
        if listed % size == 0:
            return size
    return 1


def room(*arrays):
    return sum(a.size * a.dtype.itemsize for a in arrays) + (4 << 20)


def tile_kernel(
    places, here, values_ref, *rest, flipped, in_shards, out_shards, step_blocks, group_blocks
):
    n_in = len(in_shards)
    n_out = len(out_shards)
    in_refs = rest[:n_in]
    out_refs = rest[n_in : n_in + n_out]
    stacked, acc, held, sems = rest[n_in + n_out :]
    listed, blk, _ = values_ref.shape
    steps = listed // step_blocks

    def fetch(step):
        part = pl.ds(step * step_blocks, step_blocks)
        return pltpu.make_async_copy(values_ref.at[part], held.at[part], sems.at[step])

    for step in range(steps):
        fetch(step).start()
    acc[...] = jnp.zeros_like(acc)
    for mask in sorted(set(in_shards)):
        refs = [r for r, m in zip(in_refs, in_shards) if m == mask]
        first = (here[0] ^ mask) * group_blocks
        for g in range(group_blocks):
            part = functools.reduce(jnp.add, [r[pl.ds(g * blk, blk), :] for r in refs])
            both = jnp.concatenate(halves(part), axis=1)
            stacked[first + g, 0:blk, :] = both
            stacked[first + g, blk : 2 * blk, :] = both

    def run(step, carry):
        fetch(step).wait()
        sums = []
        for q in range(step_blocks):
            k = step * step_blocks + q
            i = places[0, k]
            j = places[1, k]
            source, target = (i, j) if flipped else (j, i)
            entry = held[k]
            hi, lo = halves(entry.T if flipped else entry)
            p = jnp.dot(
                jnp.concatenate([hi, lo], axis=1), stacked[source], preferred_element_type=f32
            )
            nv = p.shape[1] // 2
            sums.append((target, p[:, :nv] + p[:, nv:]))
        for target, p in sums:
            acc[target] = acc[target] + p
        return carry

    lax.fori_loop(0, steps, run, 0)
    for ref, shards in zip(out_refs, out_shards):
        for place, mask in enumerate(shards):
            first = (here[1] ^ mask) * group_blocks
            for g in range(group_blocks):
                ref[pl.ds((place * group_blocks + g) * blk, blk), :] = acc[first + g]


def tile_products(values, places, here, pieces, in_shards, out_shards, flipped):
    listed, blk, _ = values.shape
    nv = pieces[0].shape[1]
    group = pieces[0].shape[0]
    group_blocks = group // blk
    step_blocks = chunk_of(listed)
    n_in = len(set(in_shards)) * group_blocks
    n_out = sum(len(s) for s in out_shards) * group_blocks
    vmem = pl.BlockSpec(memory_space=pltpu.VMEM)
    smem = pl.BlockSpec(memory_space=pltpu.SMEM)
    out_shape = [jax.ShapeDtypeStruct((len(s) * group, nv), f32) for s in out_shards]
    scratch = [
        jax.ShapeDtypeStruct((n_in, 2 * blk, 2 * nv), bf16),
        jax.ShapeDtypeStruct((n_out, blk, nv), f32),
        jax.ShapeDtypeStruct(values.shape, f32),
    ]
    body = functools.partial(
        tile_kernel,
        flipped=flipped,
        in_shards=in_shards,
        out_shards=out_shards,
        step_blocks=step_blocks,
        group_blocks=group_blocks,
    )
    return pl.pallas_call(
        body,
        name="tile_flipped" if flipped else "tile_direct",
        out_shape=out_shape,
        in_specs=[smem, smem, pl.BlockSpec(memory_space=pl.ANY)] + [vmem] * len(pieces),
        out_specs=[vmem] * len(out_shape),
        scratch_shapes=[pltpu.VMEM(s.shape, s.dtype) for s in scratch]
        + [pltpu.SemaphoreType.DMA((listed // step_blocks,))],
        compiler_params=pltpu.CompilerParams(vmem_limit_bytes=50 << 20),
        cost_estimate=pl.CostEstimate(
            flops=2 * listed * blk * blk * nv * 4, transcendentals=0, bytes_accessed=values.size * 4
        ),
    )(places, here, values, *pieces)


def gram_kernel(here, *rest, n_upper, n_lower, scale):
    upper_refs = rest[:n_upper]
    lower_refs = rest[n_upper : n_upper + n_lower]
    rest = rest[n_upper + n_lower :]
    if scale:
        w_ref, y_ref, mine_ref, other_ref, full = rest
    else:
        mine_ref, other_ref, full = rest
    total = None
    for band, refs in enumerate((upper_refs, lower_refs)):
        y = refs[0][...]
        for r in refs[1:]:
            y = y + r[...]
        if scale:
            y = jnp.dot(y, w_ref[...], precision=exact_mode, preferred_element_type=f32)
            y_ref[band] = y
        part = lax.dot_general(
            y, y, (((0,), (0,)), ((), ())), precision=exact_mode, preferred_element_type=f32
        )
        total = part if total is None else total + part
    full[...] = total
    half = total.shape[0] // 2
    mine_ref[...] = full[pl.ds(here[0] * half, half), :]
    other_ref[...] = full[pl.ds((1 - here[0]) * half, half), :]


def gram_parts(parity, uppers, lowers, weight=None):
    rows, nv = uppers[0].shape
    half = jax.ShapeDtypeStruct((nv // 2, nv), f32)
    out_shape = [half, half]
    args = list(uppers) + list(lowers)
    if weight is not None:
        out_shape = [jax.ShapeDtypeStruct((2, rows, nv), f32)] + out_shape
        args.append(weight)
    vmem = pl.BlockSpec(memory_space=pltpu.VMEM)
    return pl.pallas_call(
        functools.partial(
            gram_kernel, n_upper=len(uppers), n_lower=len(lowers), scale=weight is not None
        ),
        name="gram_scaled" if weight is not None else "gram_plain",
        out_shape=out_shape,
        in_specs=[pl.BlockSpec(memory_space=pltpu.SMEM)] + [vmem] * len(args),
        out_specs=[vmem] * len(out_shape),
        scratch_shapes=[pltpu.VMEM((nv, nv), f32)],
        compiler_params=pltpu.CompilerParams(vmem_limit_bytes=room(*out_shape, *args)),
    )(parity, *args)


def factor_kernel(here, *rest, n_own, total_rows, apply):
    own_refs = rest[:n_own]
    other_ref = rest[n_own]
    rest = rest[n_own + 1 :]
    if apply:
        y_ref, out_ref, full, rows, ready, sems = rest
    else:
        w_ref, full, rows = rest
    size = full.shape[0]
    half = size // 2
    own = own_refs[0][...]
    for r in own_refs[1:]:
        own = own + r[...]
    full[pl.ds(here[0] * half, half), :] = own
    full[pl.ds((1 - here[0]) * half, half), :] = other_ref[...]
    sub = 8
    groups = size // sub
    lane = lax.broadcasted_iota(jnp.int32, (sub, size), 1)
    row_in = lax.broadcasted_iota(jnp.int32, (sub, size), 0)

    def spread(x, k):
        return jnp.broadcast_to(x[:, k : k + 1], (sub, size))

    m = [full[pl.ds(g * sub, sub), :] for g in range(groups)]
    kept = [jnp.where(lane == row_in + g * sub, m[g], 0.0) for g in range(groups)]
    across = functools.reduce(jnp.add, [jnp.sum(x, axis=0, keepdims=True) for x in kept])
    inv_rows = 1.0 / total_rows
    unit_row = lax.rsqrt(across * inv_rows)
    for g in range(groups):
        unit_col = lax.rsqrt(jnp.sum(kept[g], axis=1, keepdims=True) * inv_rows)
        m[g] = (m[g] * inv_rows * unit_row) * unit_col

    for g0 in range(groups):
        k = g0 * sub
        rows[pl.ds(k, sub), :] = m[g0]
        r = [rows[pl.ds(k + i, sub, stride=0), :] for i in range(sub)]
        s = {(i, j): spread(r[i], k + j) for i in range(sub) for j in range(i, sub)}
        in_panel = (lane >= k) & (lane < k + sub)
        done = lane < k + sub
        r = [jnp.where(lane == k + i, 1.0, jnp.where(in_panel, 0.0, r[i])) for i in range(sub)]
        f = [None] * sub
        q = {}
        for i in range(0, sub, 2):
            a, b, c = s[i, i], s[i, i + 1], s[i + 1, i + 1]
            inv = 1.0 / (a * c - b * b)
            t = b / a
            first = jnp.where(done, r[i], 0.0) * lax.rsqrt(a)
            second = jnp.where(done, r[i + 1] - t * r[i], 0.0) * lax.rsqrt(c - b * t)
            full[pl.ds(k + i, 1), :] = first[0:1]
            full[pl.ds(k + i + 1, 1), :] = second[0:1]
            a, b, c = a * inv, b * inv, c * inv
            f[i] = c * r[i] - b * r[i + 1]
            f[i + 1] = a * r[i + 1] - b * r[i]
            for j in range(i + 2, sub):
                q[i, j] = c * s[i, j] - b * s[i + 1, j]
                q[i + 1, j] = a * s[i + 1, j] - b * s[i, j]
            for j in range(i + 2, sub):
                r[j] = r[j] - (s[i, j] * f[i] + s[i + 1, j] * f[i + 1])
                for l in range(j, sub):
                    s[j, l] = s[j, l] - (s[i, j] * q[i, l] + s[i + 1, j] * q[i + 1, l])
        for i in range(sub - 4, -1, -2):
            for j in range(i + 2, sub):
                f[i] = f[i] - q[i, j] * f[j]
                f[i + 1] = f[i + 1] - q[i + 1, j] * f[j]
        for g in range(g0 + 1, groups):
            change = spread(m[g], k) * f[0]
            for j in range(1, sub):
                change = change + spread(m[g], k + j) * f[j]
            m[g] = jnp.where(in_panel, 0.0, m[g]) - change

    inverse = full[...] * unit_row
    if apply:
        sends = []
        for band in range(2):
            ready[band] = lax.dot_general(
                y_ref[band],
                inverse,
                (((1,), (1,)), ((), ())),
                precision=exact_mode,
                preferred_element_type=f32,
            )
            sends.append(
                pltpu.make_async_copy(ready.at[band], out_ref.at[band], sems.at[band])
            )
            sends[-1].start()
        for send in sends:
            send.wait()
    else:
        w_ref[...] = inverse.T


def factor_inverse(parity, own, other, total_rows, applied=None):
    _, nv = other.shape
    vmem = pl.BlockSpec(memory_space=pltpu.VMEM)
    args = list(own) + [other]
    scratch = [pltpu.VMEM((nv, nv), f32), pltpu.VMEM((nv, nv), f32)]
    out_spec = vmem
    if applied is None:
        out_shape = jax.ShapeDtypeStruct((nv, nv), f32)
    else:
        out_shape = jax.ShapeDtypeStruct(applied.shape, f32)
        args.append(applied)
        scratch += [pltpu.VMEM(applied.shape, f32), pltpu.SemaphoreType.DMA((2,))]
        out_spec = pl.BlockSpec(memory_space=pl.ANY)
    return pl.pallas_call(
        functools.partial(
            factor_kernel, n_own=len(own), total_rows=total_rows, apply=applied is not None
        ),
        name="factor" if applied is None else "factor_apply",
        out_shape=out_shape,
        in_specs=[pl.BlockSpec(memory_space=pltpu.SMEM)] + [vmem] * len(args),
        out_specs=out_spec,
        scratch_shapes=scratch,
        compiler_params=pltpu.CompilerParams(vmem_limit_bytes=room(out_shape, *args)),
    )(parity, *args)


def local(blocks, coords, vectors):
    n_row = lax.axis_size("row")
    n_col = lax.axis_size("col")
    group = vectors.shape[1]
    total_rows = 2 * group * n_row * n_col
    values = blocks.reshape(blocks.shape[2], blocks.shape[3], blocks.shape[4])
    places = jnp.maximum(coords.reshape(2, coords.shape[3]), 0)
    row_id = lax.axis_index("row")
    col_id = lax.axis_index("col")
    here_direct = jnp.stack([row_id, col_id]).astype(jnp.int32)
    here_flipped = jnp.stack([col_id, row_id]).astype(jnp.int32)
    parity = (col_id & 1).astype(jnp.int32).reshape(1)
    even = list(range(2, n_col, 2))[::-1]
    row_masks = list(range(1, n_row))[::-1]

    def spread_row(x):
        if n_row != 4:
            return [x] + [swap(x, "row", m) for m in row_masks]
        two = swap(x, "row", 2)
        one = swap(x, "row", 1)
        inner = lax.ppermute(x, "row", [(1, 2), (2, 1)])
        outer = lax.ppermute(two, "row", [(1, 0), (2, 3)])
        return [x, one, two, inner, outer]

    def spread_col(x):
        far = [swap(x, "col", m) for m in even]
        near = swap(x, "col", 1)
        joined = [swap(f, "col", 1) for f in far]
        return [x, near] + far + joined

    row_in = [0, 1, 2, 3, 3] if n_row == 4 else [0] + row_masks
    row_out = [[m] for m in [0] + row_masks]
    col_in = [0, 1] + even + [m ^ 1 for m in even]
    order = even + [0]
    col_masks = [p for p in (order[: len(order) // 2], order[len(order) // 2 :]) if p]
    col_out = col_masks + [[m ^ 1 for m in p] for p in col_masks]

    def direct(pieces):
        return tile_products(values, places, here_direct, pieces, row_in, col_out, False)

    def flipped(pieces):
        return tile_products(values, places, here_flipped, pieces, col_in, row_out, True)

    def gather_col(outs):
        count = len(col_masks)
        parts = []
        for mine, others, masks in zip(outs[:count], outs[count:], col_masks):
            both = mine + swap(others, "col", 1)
            parts += [both[i * group : (i + 1) * group] for i in range(len(masks))]
        return [parts[-1]] + [swap(p, "col", m) for p, m in zip(parts, even)]

    def gather_row(outs):
        got = []
        for p, m in zip(outs[1:], row_masks):
            got.append(swap(p, "row", m))
        return [outs[0]] + got

    def reduce_gram(mine, other):
        own = mine + swap(other, "col", 1)
        own = functools.reduce(jnp.add, [own] + [swap(own, "col", m) for m in even])
        parts = [own]
        for m in row_masks:
            parts.append(swap(own, "row", m))
        own = functools.reduce(jnp.add, parts)
        return [own], swap(own, "col", 1)

    upper, lower = vectors[0], vectors[1]
    pieces_z = spread_row(lower)
    lower1 = functools.reduce(jnp.add, gather_row(flipped(spread_col(upper))))
    upper1 = functools.reduce(jnp.add, gather_col(direct(pieces_z)))
    pieces_z = spread_row(lower1)
    lowers = gather_row(flipped(spread_col(upper1)))
    parts = gram_parts(parity, [upper1], [lower1])
    parts = reduce_gram(*parts)
    weight = factor_inverse(parity, *parts, total_rows)
    uppers = gather_col(direct(pieces_z))
    applied, mine, other = gram_parts(parity, uppers, lowers, weight)
    parts = reduce_gram(mine, other)
    return factor_inverse(parity, *parts, total_rows, applied)


def solution(mesh):
    return jax.shard_map(
        local,
        mesh=mesh,
        in_specs=(
            P("row", "col", None, None, None),
            P("row", "col", None, None),
            P(None, ("row", "col"), None),
        ),
        out_specs=P(None, ("row", "col"), None),
        check_vma=False,
    )
```
